32 devices in a mesh: ev: 4 (over z), mesh: 8 (over y, x, core).
Axes of the slice: x: 2, y: 2, z: 4, core: 2. Of those that a mesh axis runs over, the one named last changes fastest.
Arguments:
- kernels: bfloat16 [8, 12, 2048, 128], P('ev', None, 'mesh'), may hold values from -6 to 6
- tile_owner: int32 [8, 4096, 1], P('ev', 'mesh'), may hold values from 0 to 7; in each aligned block of 512 rows (0 to 511, 512 to 1023, ..., all dimensions but the last counted through in order) at most 64 rows name the same one
- tile_source: int32 [8, 4096], P('ev', 'mesh'), may hold values from 0 to 255
- tile_target: int32 [8, 4096], P('ev', 'mesh'), may hold values from 0 to 31
- tile_seed: int32 [8, 4096], P('ev', 'mesh'), may hold values from 0 to 83
- tile_count: int32 [8, 8], P('ev', 'mesh'), may hold values from 256 to 512
- prev_gradient: float32 [12, 8, 32, 128], P(None, 'mesh', 'ev'), may hold values from -18 to 18
- prev_step: float32 [12, 8, 32, 128], P(None, 'mesh', 'ev'), may hold values from -18 to 18, as said below
- precond: float32 [12, 8, 32, 128], P(None, 'mesh', 'ev'), may hold values from 0.2 to 2
Outputs:
- inversion_direction: float32 [12, 8, 32, 128], P(None, 'mesh', 'ev')
- event_direction: float32 [8, 12, 2048, 128], P('ev', None, 'mesh')
The draws below stay inside these ranges and needn't reach their ends.
Inputs may be any that keep to these rules, and one draw needn't show every extreme that they name: `tile_owner`: in every aligned block of 512 rows (one event's list for one partition) no partition is named by more than 64 rows, a bound that some block reaches. Rows of a list at positions tile_count or later are padding. prev_step = -c * prev_gradient cell by cell, with c between 0.1 and 1.
All inputs are finite; a program needn't handle non-finite values.
Results may differ from the reference program's by a relative error of at most 0.0003.
The reference program's roundings to bfloat16 on the way count: a program that leaves them out, or rounds other values in their place, can miss the bound.
Values may be sent and summed in bfloat16 or wider, within the bound.
No kernel may reach another device: no remote copies, remote signals or barrier semaphores. Data moves between devices by JAX's collectives and lax.ppermute only.
A program may use at most 128 MiB of HBM per device.

```python
import math
import jax
import jax.numpy as jnp
import numpy as np
from jax import lax

C = 12
NODES = 128
EB_DEV = 256
TILES_DEV = 512
PARTITIONS = 8
EVENTS = 8
EBLOCKS = 2048
ISUB = 32
IBLOCKS = 256
CAP = 64


def history_pair(key):
    base = jax.random.fold_in(key, 11)
    first, second = jax.random.split(base)
    shape = (C, PARTITIONS, ISUB, NODES)
    older = jnp.clip(3.0 * jax.random.normal(first, shape, jnp.float32), -18.0, 18.0)
    factor = jnp.exp(jax.random.uniform(second, shape, jnp.float32, math.log(0.1), 0.0))
    return (older, -factor * older)


def draw_prev_gradient(key, part):
    return history_pair(key)[0]


def draw_prev_step(key, part):
    return history_pair(key)[1]


def place_ends(values, own_key, low, largest):
    shape = values.shape
    place = [jax.random.randint(jax.random.fold_in(own_key, axis), (), 0, shape[axis]) for axis in range(len(shape))]
    values = values.at[tuple(place)].set(low)
    longest = shape.index(max(shape))
    place[longest] = (place[longest] + 1) % shape[longest]
    return values.at[tuple(place)].set(largest)


def block_levels(stream_key, extent, shards, low, top_value):
    def one(dim, blocks):
        heights = jax.random.uniform(jax.random.fold_in(jax.random.fold_in(stream_key, 6), dim), (blocks,), jnp.float32, low / len(shards), top_value / len(shards))
        return jnp.repeat(jnp.exp(heights), extent[dim] // blocks).reshape((-1,) + (1,) * (len(extent) - dim - 1))

    gain = one(*shards[0])
    for cut in shards[1:]:
        gain = gain * one(*cut)
    return gain


def routed_block(rng, own, number, rows, count, top, most, lean):
    sequence = jax.random.permutation(rng, count)
    heavy_load, common = shares(count, rows * top, most, lean, True), shares(count, rows * top, most, lean, False)
    places = jnp.arange(count)

    def named(tallies, rotation):
        used = int((tallies > 0).sum())
        fixed = max(1, used // 4)
        passed = fixed + (places - fixed + rotation * (used - fixed)) % max(1, count - fixed)
        return jnp.zeros((count,), jnp.int32).at[sequence[jnp.where(places < fixed, places, passed)]].set(jnp.asarray(tallies, jnp.int32))

    tallies = jnp.where(number % 4 == 0, named(heavy_load, number // 4), named(common, number - number // 4 - 1))
    mixed = jax.random.permutation(jax.random.fold_in(own, 3), count)
    source_of, taker = mixed[0:count // 2 * 2:2], mixed[1:count // 2 * 2:2]
    margin = jnp.minimum(tallies[source_of] - 1, most - tallies[taker]) // 2
    margin = jnp.where((source_of == sequence[0]) | (taker == sequence[0]) | (tallies[taker] == 0), 0, jnp.maximum(margin, 0))
    passed = jax.random.randint(jax.random.fold_in(own, 4), (count // 2,), 0, 1 << 20) % (margin + 1)
    tallies = tallies.at[source_of].add(-passed).at[taker].add(passed)
    items = jnp.searchsorted(jnp.cumsum(tallies), jnp.arange(rows * top), side="right").astype(jnp.int32)
    listing = items.reshape(top, rows).T
    listing = listing[jax.random.permutation(jax.random.fold_in(own, 1), rows)]
    rotation = jax.random.randint(jax.random.fold_in(own, 2), (rows, 1), 0, top)
    return jnp.take_along_axis(listing, (jnp.arange(top)[None, :] + rotation) % top, axis=1)


def shares(number_of, total, most, slope, full):
    weights = [(1 << 20) // math.isqrt(rank ** slope) + 1 for rank in range(1, number_of + 1)]
    largest = most if full else min(most, max(-(-total // number_of), total * weights[0] // sum(weights)))
    least = 1 if total - largest >= number_of - 1 else 0
    counts, surplus = [largest] + [least] * (number_of - 1), total - largest - least * (number_of - 1)
    while surplus > 0:
        free = [i for i in range(1, number_of) if counts[i] < largest] or [i for i in range(1, number_of) if counts[i] < most]
        pool, left = sum([weights[i] for i in free]), surplus
        for i in free:
            addition = min(most - counts[i], max(1, left * weights[i] // pool), surplus)
            counts[i] = counts[i] + addition
            surplus = surplus - addition
    return np.array(counts)


def bell_draw(key, extent, deviation, most, cuts=(), kind=jnp.bfloat16):
    values = jax.random.normal(key, extent, jnp.float32) * deviation
    if len(cuts) > 0:
        values = block_levels(key, extent, cuts, -0.22, 0.18) * values
    return jnp.clip(values, min=-most, max=most).astype(kind)


def setup_inputs(seed: int = 0) -> dict:
    keys = jax.random.split(jax.random.key(seed), 10)
    kernels = bell_draw(keys[0], (EVENTS, C, EBLOCKS, NODES), 1.0, 6.0, ((0, 4), (2, 8)))
    tile_owner_keys = jax.random.split(jax.random.fold_in(keys[1], 1), EVENTS * (PARTITIONS * TILES_DEV) // TILES_DEV)
    tile_owner_turns = jax.random.permutation(jax.random.fold_in(keys[1], 3), EVENTS * (PARTITIONS * TILES_DEV) // TILES_DEV)
    tile_owner = jax.vmap(lambda own, number: routed_block(jax.random.fold_in(keys[1], 2), own, number, TILES_DEV, PARTITIONS, 1, CAP, 2))(tile_owner_keys, tile_owner_turns).reshape((EVENTS, PARTITIONS * TILES_DEV, 1))
    tile_source = place_ends(jax.random.randint(keys[2], (EVENTS, PARTITIONS * TILES_DEV), 0, EB_DEV), jax.random.fold_in(keys[2], 1), 0, EB_DEV - 1).astype(jnp.int32)
    tile_target = place_ends(jax.random.randint(keys[3], (EVENTS, PARTITIONS * TILES_DEV), 0, ISUB), jax.random.fold_in(keys[3], 1), 0, ISUB - 1).astype(jnp.int32)
    tile_seed = place_ends(jax.random.randint(keys[4], (EVENTS, PARTITIONS * TILES_DEV), 0, 84), jax.random.fold_in(keys[4], 1), 0, 83).astype(jnp.int32)
    tile_count = place_ends(jax.random.randint(keys[5], (EVENTS, PARTITIONS), TILES_DEV // 2, TILES_DEV + 1), jax.random.fold_in(keys[5], 1), TILES_DEV // 2, TILES_DEV).astype(jnp.int32)
    prev_gradient = draw_prev_gradient(jax.random.fold_in(keys[9], 71), 0)
    prev_step = draw_prev_step(jax.random.fold_in(keys[9], 71), 0)
    precond = jnp.clip(jnp.exp(math.log(2.0) - 2.3025851 * jax.random.uniform(keys[8], (C, PARTITIONS, ISUB, NODES), jnp.float32) ** block_levels(keys[8], (C, PARTITIONS, ISUB, NODES), ((1, 8), (2, 4)), -0.2, 0.2)), 0.2, 2.0)
    return dict(kernels=kernels, tile_owner=tile_owner, tile_source=tile_source, tile_target=tile_target, tile_seed=tile_seed, tile_count=tile_count, prev_gradient=prev_gradient, prev_step=prev_step, precond=precond)


def make_tiles(seed_ids):
    node_pos = jnp.arange(NODES).astype(jnp.float32)
    seed_ids = seed_ids.astype(jnp.int32)
    offset = (seed_ids % 7 - 3).astype(jnp.float32)
    spread = 0.55 + 0.1 * ((seed_ids // 7) % 3).astype(jnp.float32)
    weight = 0.1 + 0.1 * (seed_ids // 21).astype(jnp.float32)
    distance = node_pos[None, :, None] - node_pos[None, None, :] - offset[:, None, None]
    values = weight[:, None, None] * jnp.exp(-distance * distance / (2.0 * spread * spread)[:, None, None])
    return values.astype(jnp.bfloat16)


def reference(kernels, tile_owner, tile_source, tile_target, tile_seed, tile_count, prev_gradient, prev_step, precond):
    groups = EVENTS * PARTITIONS
    owner_ids = tile_owner.reshape(groups, TILES_DEV).astype(jnp.int32)
    source_ids = tile_source.reshape(groups, TILES_DEV).astype(jnp.int32)
    target_ids = tile_target.reshape(groups, TILES_DEV).astype(jnp.int32)
    seed_ids = tile_seed.reshape(groups, TILES_DEV).astype(jnp.int32)
    limits = tile_count.reshape(groups).astype(jnp.int32)
    group_ids = jnp.arange(groups, dtype=jnp.int32)
    group_event = group_ids // PARTITIONS
    group_part = group_ids % PARTITIONS
    position = jnp.arange(TILES_DEV, dtype=jnp.int32)

    def forward(total, inputs):
        owners, sources, targets, seeds, event, part, limit = inputs
        field = lax.dynamic_index_in_dim(kernels, event, 0, keepdims=False)
        picked = jnp.transpose(field[:, part * EB_DEV + sources, :], (1, 0, 2))
        tile_mats = make_tiles(seeds)
        product = jnp.einsum('tcn,tnm->tcm', picked.astype(jnp.float32), tile_mats.astype(jnp.float32))
        live_mask = (position < limit).astype(jnp.float32)
        contribution = (product * live_mask[:, None, None]).astype(jnp.bfloat16)
        blocks = owners * ISUB + targets
        added = jax.ops.segment_sum(contribution.astype(jnp.float32), blocks, num_segments=IBLOCKS)
        return total + added, None

    start = jnp.zeros((IBLOCKS, C, NODES), jnp.float32)
    summed, _ = lax.scan(forward, start, (owner_ids, source_ids, target_ids, seed_ids, group_event, group_part, limits))
    gradient = jnp.transpose(summed.reshape(PARTITIONS, ISUB, C, NODES), (2, 0, 1, 3))

    change = gradient - prev_gradient
    curvature = jnp.sum(prev_step * change)
    alpha = jnp.sum(prev_step * gradient) / curvature
    scaled = precond * (gradient - alpha * change)
    beta = jnp.sum(change * scaled) / curvature
    inversion_direction = -(scaled + (alpha - beta) * prev_step)

    rounded = inversion_direction.astype(jnp.bfloat16)
    flat_direction = jnp.transpose(rounded.reshape(C, IBLOCKS, NODES), (1, 0, 2))

    def per_event(event):
        def backward(total, part):
            group = event * PARTITIONS + part
            owners = lax.dynamic_index_in_dim(owner_ids, group, 0, keepdims=False)
            sources = lax.dynamic_index_in_dim(source_ids, group, 0, keepdims=False)
            targets = lax.dynamic_index_in_dim(target_ids, group, 0, keepdims=False)
            seeds = lax.dynamic_index_in_dim(seed_ids, group, 0, keepdims=False)
            limit = lax.dynamic_index_in_dim(limits, group, 0, keepdims=False)
            picked = flat_direction[owners * ISUB + targets]
            tile_mats = make_tiles(seeds)
            product = jnp.einsum('tcm,tnm->tcn', picked.astype(jnp.float32), tile_mats.astype(jnp.float32))
            live_mask = (position < limit).astype(jnp.float32)
            product = product * live_mask[:, None, None]
            added = jax.ops.segment_sum(product, part * EB_DEV + sources, num_segments=EBLOCKS)
            return total + added, None

        empty = jnp.zeros((EBLOCKS, C, NODES), jnp.float32)
        result, _ = lax.scan(backward, empty, jnp.arange(PARTITIONS, dtype=jnp.int32))
        return jnp.transpose(result, (1, 0, 2))

    event_direction = lax.map(per_event, jnp.arange(EVENTS, dtype=jnp.int32))
    return inversion_direction, event_direction
```

```python
import functools

import jax
import jax.numpy as jnp
import numpy as np
from jax import lax
from jax.experimental import pallas as pl
from jax.experimental.pallas import tpu as pltpu
from jax.sharding import PartitionSpec as P

OFFSETS = 7
SPREADS = 3
WEIGHTS = 4
SHAPES = OFFSETS * SPREADS * WEIGHTS
ROW = 16
UNROLL = 8


def fill_table(tab_ref, nodes):
    row = lax.broadcasted_iota(jnp.int32, (nodes, nodes), 0)
    col = lax.broadcasted_iota(jnp.int32, (nodes, nodes), 1)
    gap = (row - col).astype(jnp.float32)

    def one(k, carry):
        offset = (k % OFFSETS - OFFSETS // 2).astype(jnp.float32)
        spread = 0.55 + 0.1 * (k // OFFSETS).astype(jnp.float32)
        distance = gap - offset
        bell = jnp.exp(-distance * distance / (2.0 * spread * spread))
        for w in range(WEIGHTS):
            weight = np.float32(0.1) + np.float32(0.1) * np.float32(w)
            at = pl.multiple_of((w * OFFSETS * SPREADS + k) * nodes, nodes)
            tab_ref[pl.ds(at, nodes), :] = (weight * bell).astype(jnp.bfloat16)
        return carry

    lax.fori_loop(0, OFFSETS * SPREADS, one, 0)


def tile_loop(count, unroll, one):
    def group(i, carry):
        for u in range(unroll):
            one(i * unroll + u, u)
        return carry

    lax.fori_loop(0, (count + unroll - 1) // unroll, group, 0)


def forward_kernel(
    dims, base_ref, count_ref, source_ref, block_ref, seed_ref, field_ref, keep_ref, send_ref,
    tab_ref, rows_ref, sum_a, sum_b,
):
    events, comps, eblocks, nodes, tiles, blocks, group = dims
    fill_table(tab_ref, nodes)
    sum_a[...] = jnp.zeros_like(sum_a)
    sum_b[...] = jnp.zeros_like(sum_b)
    for v in range(events):
        for c in range(comps):
            rows_ref[pl.ds(v * eblocks * ROW + c, eblocks, stride=ROW), :] = field_ref[
                v, c
            ].astype(jnp.float32)
    for v in range(events):
        count = count_ref[v]

        def one(t, u, v=v, count=count):
            at = v * tiles + t
            src = pl.multiple_of(source_ref[at] * ROW + v * eblocks * ROW, ROW)
            block = jnp.where(t < count, block_ref[at], blocks)
            shape = pl.multiple_of(seed_ref[at] * nodes, nodes)
            x = rows_ref[pl.ds(src, ROW), :].astype(jnp.bfloat16)
            y = jnp.dot(x, tab_ref[pl.ds(shape, nodes), :], preferred_element_type=jnp.float32)
            y = y.astype(jnp.bfloat16).astype(jnp.float32)
            total = sum_a if u % 2 == 0 else sum_b
            to = pl.ds(pl.multiple_of(block * ROW, ROW), ROW)
            total[to, :] = total[to, :] + y

        tile_loop(count, UNROLL, one)
    chunks = keep_ref.shape[0]
    for half, out_ref in enumerate((keep_ref, send_ref)):

        def put(j, carry, half=half, out_ref=out_ref):
            first = base_ref[half * chunks + j] * ROW
            for c in range(comps):
                at = pl.ds(first + c, group, stride=ROW)
                out_ref[j, pl.ds(c * group, group), :] = sum_a[at, :] + sum_b[at, :]
            return carry

        lax.fori_loop(0, chunks, put, 0)


def backward_kernel(
    dims, base_ref, count_ref, source_ref, block_ref, seed_ref, mine_ref, other_ref, out_ref,
    tab_ref, rows_ref, sum_ref,
):
    events, comps, eblocks, nodes, tiles, blocks, group = dims
    fill_table(tab_ref, nodes)
    sum_ref[...] = jnp.zeros_like(sum_ref)
    chunks = mine_ref.shape[0]
    for half, in_ref in enumerate((mine_ref, other_ref)):

        def take(j, carry, half=half, in_ref=in_ref):
            first = base_ref[half * chunks + j] * ROW
            values = in_ref[j].astype(jnp.float32)
            for c in range(comps):
                rows_ref[pl.ds(first + c, group, stride=ROW), :] = values[
                    c * group : (c + 1) * group
                ]
            return carry

        lax.fori_loop(0, chunks, take, 0)
    for v in range(events):
        count = count_ref[v]

        def one(t, u, v=v, count=count):
            at = v * tiles + t
            src = jnp.where(t < count, source_ref[at] + v * eblocks, events * eblocks)
            seed = seed_ref[at]
            shape = pl.multiple_of(seed * nodes, nodes)
            x = rows_ref[pl.ds(pl.multiple_of(block_ref[at] * ROW, ROW), ROW), :]
            y = jnp.dot(
                x.astype(jnp.bfloat16),
                tab_ref[pl.ds(shape, nodes), :],
                preferred_element_type=jnp.float32,
            )
            to = pl.ds(pl.multiple_of(src * ROW, ROW), ROW)
            sum_ref[to, :] = sum_ref[to, :] + y

        tile_loop(count, UNROLL, one)
    for v in range(events):
        for c in range(comps):
            out_ref[v, c] = sum_ref[pl.ds(v * eblocks * ROW + c, eblocks, stride=ROW), :]


def smem():
    return pl.BlockSpec(memory_space=pltpu.SMEM)


def vmem():
    return pl.BlockSpec(memory_space=pltpu.VMEM)


def body(
    kernels, tile_owner, tile_source, tile_target, tile_seed, tile_count, prev_gradient,
    prev_step, precond,
):
    events, comps, eblocks, nodes = kernels.shape
    tiles = tile_source.shape[1]
    parts = lax.axis_size("mesh")
    evs = lax.axis_size("ev")
    group = precond.shape[2]
    subs = group * evs
    blocks = parts * subs
    bits = parts.bit_length() - 1
    me = lax.axis_index("mesh")
    ev = lax.axis_index("ev")
    dims = (events, comps, eblocks, nodes, tiles, blocks, group)
    half = parts // 2

    def relation(odd, j):
        r = j << 1
        if bits < 3:
            return jnp.full_like(odd, r)
        a, b = (r >> 1) & 1, (r >> 2) & 1
        swapped = (r & ~6) | (a << 2) | (b << 1)
        return jnp.where(odd == 1, swapped, r)

    def bit_of(odd, step):
        if bits < 3 or step not in (1, 2):
            return 1 << step
        return (1 << (3 - step)) if odd else (1 << step)

    def swap(x, step):
        pairs = [(i, i ^ bit_of(i & 1, step)) for i in range(parts)]
        return lax.ppermute(x, "mesh", pairs)

    ev_slots = [jnp.remainder(ev + k, evs) for k in range(evs)]

    def slot_bases(device, odd):
        return [
            (device ^ relation(odd, j)) * subs + ev_slots[k] * group
            for j in range(half)
            for k in range(evs)
        ]

    odd = me & 1
    mine = slot_bases(me, odd)
    other = slot_bases(me ^ 1, 1 - odd)
    bases = jnp.stack(mine + other).astype(jnp.int32)

    block_ids = (tile_owner.reshape(events, tiles) * subs + tile_target).reshape(events * tiles)
    source_ids = tile_source.reshape(events * tiles)
    seed_ids = tile_seed.reshape(events * tiles)
    turned = seed_ids - 2 * (seed_ids % OFFSETS) + (OFFSETS - 1)
    counts = tile_count.reshape(events)
    chunks = half * evs
    chunk_rows = comps * group

    keep, send = pl.pallas_call(
        functools.partial(forward_kernel, dims),
        out_shape=[jax.ShapeDtypeStruct((chunks, chunk_rows, nodes), jnp.float32)] * 2,
        in_specs=[smem()] * 5 + [vmem()],
        out_specs=[vmem()] * 2,
        scratch_shapes=[
            pltpu.VMEM((SHAPES * nodes, nodes), jnp.bfloat16),
            pltpu.VMEM((events * eblocks * ROW, nodes), jnp.float32),
            pltpu.VMEM(((blocks + 1) * ROW, nodes), jnp.float32),
            pltpu.VMEM(((blocks + 1) * ROW, nodes), jnp.float32),
        ],
        name="forward",
    )(bases, counts, source_ids, block_ids, seed_ids, kernels)

    got = swap(send, 0)
    held = keep + got
    slots = half
    for step in range(1, bits):
        view = held.reshape(slots // 2, 2, evs, chunk_rows, nodes)
        got = swap(view[:, 1], step)
        held = (view[:, 0] + got).reshape(slots // 2 * evs, chunk_rows, nodes)
        slots //= 2
    held = held.reshape(evs, chunk_rows, nodes)
    total = held[0]
    for k in range(1, evs):
        total = total + lax.ppermute(held[k], "ev", [(i, (i + k) % evs) for i in range(evs)])
    gradient = total.reshape(comps, 1, group, nodes)

    change = gradient - prev_gradient
    weighted = precond * change
    local = jnp.stack(
        [
            jnp.sum(prev_step * change),
            jnp.sum(prev_step * gradient),
            jnp.sum(weighted * gradient),
            jnp.sum(weighted * change),
        ]
    )
    spread = jnp.broadcast_to(jnp.pad(local, (0, nodes - 4))[None, :], (parts * evs, nodes))
    sums = jnp.sum(lax.all_to_all(spread, ("ev", "mesh"), 0, 0, tiled=True), axis=0)
    curvature, slope, cross_term, self_term = sums[0], sums[1], sums[2], sums[3]
    alpha = slope / curvature
    scaled = precond * (gradient - alpha * change)
    beta = (cross_term - alpha * self_term) / curvature
    inversion_direction = -(scaled + (alpha - beta) * prev_step)
    rounded = inversion_direction.astype(jnp.bfloat16).reshape(chunk_rows, nodes)

    pieces = [rounded] + [
        lax.ppermute(rounded, "ev", [(i, (i - k) % evs) for i in range(evs)])
        for k in range(1, evs)
    ]
    gathered = jnp.stack(pieces)[None]
    for step in reversed(range(1, bits)):
        gathered = jnp.stack([gathered, swap(gathered, step)], axis=1)
        gathered = gathered.reshape((-1,) + gathered.shape[2:])
    gathered = gathered.reshape(chunks, chunk_rows, nodes)
    partner = swap(gathered, 0)

    event_direction = pl.pallas_call(
        functools.partial(backward_kernel, dims),
        out_shape=jax.ShapeDtypeStruct((events, comps, eblocks, nodes), jnp.float32),
        in_specs=[smem()] * 5 + [vmem()] * 2,
        out_specs=vmem(),
        scratch_shapes=[
            pltpu.VMEM((SHAPES * nodes, nodes), jnp.bfloat16),
            pltpu.VMEM(((blocks + 1) * ROW, nodes), jnp.float32),
            pltpu.VMEM(((events * eblocks + 1) * ROW, nodes), jnp.float32),
        ],
        name="backward",
    )(bases, counts, source_ids, block_ids, turned, gathered, partner)
    return inversion_direction, event_direction


def solution(mesh):
    in_specs = (
        P("ev", None, "mesh", None),
        P("ev", "mesh", None),
        P("ev", "mesh"),
        P("ev", "mesh"),
        P("ev", "mesh"),
        P("ev", "mesh"),
        P(None, "mesh", "ev", None),
        P(None, "mesh", "ev", None),
        P(None, "mesh", "ev", None),
    )
    out_specs = (P(None, "mesh", "ev", None), P("ev", None, "mesh", None))
    return jax.shard_map(body, mesh=mesh, in_specs=in_specs, out_specs=out_specs, check_vma=False)
```

```python
import functools

import jax
import jax.numpy as jnp
import numpy as np
from jax import lax
from jax.experimental import pallas as pl
from jax.experimental.pallas import tpu as pltpu
from jax.sharding import PartitionSpec as P

OFFSETS = 7
SPREADS = 3
WEIGHTS = 4
SHAPES = OFFSETS * SPREADS * WEIGHTS
ROW = 16
LANES = 128
BAND = 16
BODY = 64


def fill_table(tab_ref, nodes):
    row = lax.broadcasted_iota(jnp.int32, (8, nodes), 0)
    lane = lax.broadcasted_iota(jnp.int32, (8, nodes), 1)
    signed = jnp.where(lane < nodes // 2, lane, lane - nodes)

    def one(k, carry):
        offset = k % OFFSETS - OFFSETS // 2
        spread = 0.55 + 0.1 * (k // OFFSETS).astype(jnp.float32)
        wrapped = row - signed - offset
        distance = wrapped.astype(jnp.float32)
        base = jnp.exp(-distance * distance / (2.0 * spread * spread))
        bells = []
        for i in range(0, nodes, 8):
            bell = base if i == 0 else pltpu.roll(base, i, 1)
            if i < 2 * BAND or i >= nodes - 2 * BAND:
                near = jnp.abs(row + i - lane) < nodes // 2
                bell = jnp.where(near, bell, 0.0)
            bells.append(bell)
        for w in range(WEIGHTS):
            weight = np.float32(0.1) + np.float32(0.1) * np.float32(w)
            at = pl.multiple_of((w * OFFSETS * SPREADS + k) * nodes, nodes)
            for i in range(0, len(bells), 2):
                pair = jnp.concatenate([weight * bells[i], weight * bells[i + 1]], axis=0)
                tab_ref[pl.ds(at + i * 8, 16), :] = pair.astype(jnp.bfloat16)
        return carry

    lax.fori_loop(0, OFFSETS * SPREADS, one, 0)


def tile_loop(count, load, add):
    def group(i, carry):
        results = []
        for u in range(0, BODY, 2):
            x0, g0 = load(i * BODY + u)
            x1, g1 = load(i * BODY + u + 1)
            y = jnp.dot(
                jnp.concatenate([x0, x1], axis=0),
                jnp.concatenate([g0, g1], axis=1),
                preferred_element_type=jnp.float32,
            )
            results += [y[:ROW, :LANES], y[ROW:, LANES:]]
        for u in range(BODY):
            add(i * BODY + u, results[u])
        return carry

    lax.fori_loop(0, (count + BODY - 1) // BODY, group, 0)


def slot_of(dims, owner, target):
    half, subs = dims["half"], dims["subs"]
    r = lax.axis_index("mesh") ^ owner
    return ((r & 1) * half + (r >> 1)) * subs + target


def forward_kernel(
    dims, count_ref, owner_ref, target_ref, source_ref, seed_ref, field_ref,
    sum_ref, tab_out, tab_ref, raw_ref, rows_ref, sems,
):
    events, comps, eblocks, nodes = dims["field"]
    blocks = dims["blocks"]
    fetch = pltpu.make_async_copy(field_ref, raw_ref, sems.at[0])
    fetch.start()
    fill_table(tab_ref, nodes)
    hand_on = pltpu.make_async_copy(tab_ref, tab_out, sems.at[1])
    sum_ref[...] = jnp.zeros_like(sum_ref)
    fetch.wait()
    for v in range(events):
        for c in range(comps):
            rows_ref[pl.ds(v * eblocks * ROW + c, eblocks, stride=ROW), :] = raw_ref[
                v, c
            ].astype(jnp.float32)
    hand_on.start()
    for v in range(events):
        count = count_ref[v, 0]

        def load(t, v=v):
            src = pl.multiple_of(source_ref[v, t] * ROW + v * eblocks * ROW, ROW)
            shape = pl.multiple_of(seed_ref[v, t] * nodes, nodes)
            return rows_ref[pl.ds(src, ROW), :].astype(jnp.bfloat16), tab_ref[pl.ds(shape, nodes), :]

        def add(t, y, v=v, count=count):
            slot = slot_of(dims, owner_ref[v, 0, t], target_ref[v, t])
            at = pl.ds(pl.multiple_of(jnp.where(t < count, slot, blocks) * comps, 4), comps)
            y = y.astype(jnp.bfloat16).astype(jnp.float32)
            sum_ref[at, :] = sum_ref[at, :] + y[:comps]

        tile_loop(count, load, add)
    hand_on.wait()


def backward_kernel(
    dims, count_ref, owner_ref, target_ref, source_ref, seed_ref, tab_in, *refs,
):
    events, comps, eblocks, nodes = dims["field"]
    half, subs = dims["half"], dims["subs"]
    mine_refs, (other_ref, out_ref, tab_ref, rows_ref, sum_ref, tile_ref, sems) = (
        refs[:half], refs[half:],
    )
    fetch = pltpu.make_async_copy(tab_in, tab_ref, sems.at[0])
    fetch.start()
    sum_ref[...] = jnp.zeros_like(sum_ref)
    part = subs * comps
    for j in range(half):
        rows_ref[pl.ds(j * part, part), :] = mine_refs[j][...].astype(jnp.float32)
        rows_ref[pl.ds((half + j) * part, part), :] = other_ref[j].astype(jnp.float32)
    fetch.wait()
    sends = []
    for v in range(events):
        count = count_ref[v, 0]

        def load(t, v=v):
            slot = slot_of(dims, owner_ref[v, 0, t], target_ref[v, t])
            seed = seed_ref[v, t]
            turned = seed - 2 * lax.rem(seed, OFFSETS) + (OFFSETS - 1)
            shape = pl.multiple_of(turned * nodes, nodes)
            at = pl.ds(pl.multiple_of(slot * comps, 4), ROW)
            return rows_ref[at, :].astype(jnp.bfloat16), tab_ref[pl.ds(shape, nodes), :]

        def add(t, y, v=v, count=count):
            src = jnp.where(t < count, source_ref[v, t] + v * eblocks, events * eblocks)
            at = pl.ds(pl.multiple_of(src * ROW, ROW), ROW)
            sum_ref[at, :] = sum_ref[at, :] + y

        tile_loop(count, load, add)
        for c in range(comps):
            tile_ref[v, c] = sum_ref[pl.ds(v * eblocks * ROW + c, eblocks, stride=ROW), :]
        send = pltpu.make_async_copy(tile_ref.at[v], out_ref.at[v], sems.at[1 + v])
        send.start()
        sends.append(send)
    for send in sends:
        send.wait()


def pack_kernel(comps, group, *refs):
    ins, (out_ref, wide_ref) = refs[:-2], refs[-2:]
    rows = comps * group
    for n, ref in enumerate(ins):
        for c in range(comps):
            wide_ref[pl.ds(c, group, stride=ROW), :] = ref[c, 0]
        for s in range(group):
            out_ref[n, pl.ds(s * comps, comps), :] = wide_ref[pl.ds(s * ROW, comps), :]


def terms(a_ref, b_ref, hist_ref, k, rows, evs):
    group = lax.axis_index("ev") ^ k
    at = pl.ds(pl.multiple_of(group * rows, 8), rows)
    gradient = a_ref[at, :] + b_ref[at, :]
    prev_gradient, prev_step, precond = hist_ref[k, 0], hist_ref[k, 1], hist_ref[k, 2]
    return at, gradient, gradient - prev_gradient, prev_step, precond


def sums_kernel(rows, evs, a_ref, b_ref, hist_ref, out_ref):
    total = [jnp.zeros((8, LANES), jnp.float32) for _ in range(4)]
    for k in range(evs):
        _, gradient, change, prev_step, precond = terms(a_ref, b_ref, hist_ref, k, rows, evs)
        weighted = precond * change
        parts = (prev_step * change, prev_step * gradient, weighted * gradient, weighted * change)
        for n, part in enumerate(parts):
            total[n] = total[n] + jnp.sum(part.reshape(rows // 8, 8, LANES), axis=0)
    for n in range(4):
        out_ref[pl.ds(n, 1), :] = jnp.sum(total[n], axis=0, keepdims=True)
    out_ref[pl.ds(4, 4), :] = jnp.zeros((4, LANES), jnp.float32)


def direction_kernel(rows, evs, comps, group, a_ref, b_ref, hist_ref, *refs):
    sum_refs, (inv_ref, round_ref, wide_ref) = refs[:-3], refs[-3:]
    level = [ref[...] for ref in sum_refs]
    while len(level) > 1:
        level = [level[i] + level[i + 1] for i in range(0, len(level), 2)]
    sums = jnp.sum(level[0], axis=1, keepdims=True)
    curvature, slope, cross_term, self_term = (sums[n : n + 1] for n in range(4))
    alpha = slope / curvature
    beta = (cross_term - alpha * self_term) / curvature
    bend = alpha - beta
    for k in range(evs):
        at, gradient, change, prev_step, precond = terms(a_ref, b_ref, hist_ref, k, rows, evs)
        scaled = precond * (gradient - alpha * change)
        direction = -(scaled + bend * prev_step)
        round_ref[at, :] = direction.astype(jnp.bfloat16)
        if k == 0:
            for s in range(group):
                wide_ref[pl.ds(s * ROW, comps), :] = direction[s * comps : (s + 1) * comps]
            for c in range(comps):
                inv_ref[c, 0] = wide_ref[pl.ds(c, group, stride=ROW), :]


def in_smem():
    return pl.BlockSpec(memory_space=pltpu.SMEM)


def in_vmem():
    return pl.BlockSpec(memory_space=pltpu.VMEM)


def in_place():
    return pl.BlockSpec(memory_space=pl.ANY)


def limit(mib):
    return pltpu.CompilerParams(vmem_limit_bytes=mib << 20)


def f32(*shape):
    return jax.ShapeDtypeStruct(shape, jnp.float32)


def bf16(*shape):
    return jax.ShapeDtypeStruct(shape, jnp.bfloat16)


def body(
    kernels, tile_owner, tile_source, tile_target, tile_seed, tile_count, prev_gradient,
    prev_step, precond,
):
    events, comps, eblocks, nodes = kernels.shape
    parts = lax.axis_size("mesh")
    evs = lax.axis_size("ev")
    group = precond.shape[2]
    subs = group * evs
    blocks = parts * subs
    half = parts // 2
    rows = comps * group
    part_rows = comps * subs
    dims = dict(field=kernels.shape, half=half, subs=subs, blocks=blocks)

    def swap(x, axis, k):
        size = parts if axis == "mesh" else evs
        return lax.ppermute(x, axis, [(i, i ^ k) for i in range(size)])

    owners = jnp.transpose(tile_owner, (0, 2, 1))
    lists = (tile_count, owners, tile_target, tile_source, tile_seed)
    table = bf16(SHAPES * nodes, nodes)

    packed = pl.pallas_call(
        functools.partial(pack_kernel, comps, group),
        out_shape=f32(3, rows, nodes),
        in_specs=[in_vmem()] * 3,
        out_specs=in_vmem(),
        scratch_shapes=[pltpu.VMEM((group * ROW, nodes), jnp.float32)],
        compiler_params=limit(2),
        name="pack",
    )(prev_gradient, prev_step, precond)

    sums, tab = pl.pallas_call(
        functools.partial(forward_kernel, dims),
        out_shape=[f32(blocks * comps + ROW, nodes), table],
        in_specs=[in_smem()] * 5 + [in_place()],
        out_specs=[in_vmem(), in_place()],
        scratch_shapes=[
            pltpu.VMEM(table.shape, jnp.bfloat16),
            pltpu.VMEM(kernels.shape, jnp.bfloat16),
            pltpu.VMEM((events * eblocks * ROW, nodes), jnp.float32),
            pltpu.SemaphoreType.DMA((2,)),
        ],
        compiler_params=limit(20),
        name="forward",
    )(*lists, kernels)

    hist = packed[None]
    for bit in range(evs.bit_length() - 1):
        hist = jnp.concatenate([hist, swap(hist, "ev", 1 << bit)], axis=0)

    keep = sums[: half * part_rows].reshape(half, part_rows, nodes)
    send = sums[half * part_rows : 2 * half * part_rows].reshape(half, part_rows, nodes)
    got = swap(send, "mesh", 1)
    held = [keep[j] + got[j] for j in range(half)]
    arrived = [swap(held[j], "mesh", 2 * j) for j in range(1, half)]
    total = held[0]
    for piece in arrived:
        total = total + piece
    bits = evs.bit_length() - 1
    for bit in range(bits - 1):
        total = total + swap(total, "ev", 1 << bit)
    across = swap(total, "ev", 1 << (bits - 1))

    local = pl.pallas_call(
        functools.partial(sums_kernel, rows, evs),
        out_shape=f32(8, nodes),
        in_specs=[in_vmem()] * 3,
        out_specs=in_vmem(),
        compiler_params=limit(4),
        name="sums",
    )(total, across, hist)
    local = local + swap(local, "mesh", 1)
    spread = [local] + [swap(local, "mesh", 2 * j) for j in range(1, half)]
    inversion_direction, rounded = pl.pallas_call(
        functools.partial(direction_kernel, rows, evs, comps, group),
        out_shape=[f32(*precond.shape), bf16(part_rows, nodes)],
        in_specs=[in_vmem()] * (3 + half),
        out_specs=[in_vmem()] * 2,
        scratch_shapes=[pltpu.VMEM((group * ROW, nodes), jnp.float32)],
        compiler_params=limit(4),
        name="direction",
    )(total, across, hist, *spread)

    mine = [rounded] + [swap(rounded, "mesh", 2 * j) for j in range(1, half)]
    other = swap(jnp.stack(mine), "mesh", 1)

    event_direction = pl.pallas_call(
        functools.partial(backward_kernel, dims),
        out_shape=f32(*kernels.shape),
        in_specs=[in_smem()] * 5 + [in_place()] + [in_vmem()] * (half + 1),
        out_specs=in_place(),
        scratch_shapes=[
            pltpu.VMEM(table.shape, jnp.bfloat16),
            pltpu.VMEM((blocks * comps + ROW, nodes), jnp.float32),
            pltpu.VMEM(((events * eblocks + 1) * ROW, nodes), jnp.float32),
            pltpu.VMEM(kernels.shape, jnp.float32),
            pltpu.SemaphoreType.DMA((1 + events,)),
        ],
        compiler_params=limit(24),
        name="backward",
    )(*lists, tab, *mine, other)
    return inversion_direction, event_direction


def solution(mesh):
    in_specs = (
        P("ev", None, "mesh", None),
        P("ev", "mesh", None),
        P("ev", "mesh"),
        P("ev", "mesh"),
        P("ev", "mesh"),
        P("ev", "mesh"),
        P(None, "mesh", "ev", None),
        P(None, "mesh", "ev", None),
        P(None, "mesh", "ev", None),
    )
    out_specs = (P(None, "mesh", "ev", None), P("ev", None, "mesh", None))
    return jax.shard_map(body, mesh=mesh, in_specs=in_specs, out_specs=out_specs, check_vma=False)
```

```python
import functools

import jax
import jax.numpy as jnp
import numpy as np
from jax import lax
from jax.experimental import pallas as pl
from jax.experimental.pallas import tpu as pltpu
from jax.sharding import PartitionSpec as P

OFFSETS = 7
SPREADS = 3
WEIGHTS = 4
SHAPES = OFFSETS * SPREADS * WEIGHTS
ROW = 16
PITCH = 13
LANES = 128
BAND = 16
CODES = 4


def fill_table(tab_ref, nodes):
    row = lax.broadcasted_iota(jnp.int32, (8, nodes), 0)
    lane = lax.broadcasted_iota(jnp.int32, (8, nodes), 1)
    signed = jnp.where(lane < nodes // 2, lane, lane - nodes)

    def one(k, carry):
        spread = 0.55 + 0.1 * k.astype(jnp.float32)
        for o in range(OFFSETS):
            distance = (row - signed - (o - OFFSETS // 2)).astype(jnp.float32)
            base = jnp.exp(-distance * distance / (2.0 * spread * spread))
            bells = []
            for i in range(0, nodes, 8):
                bell = base if i == 0 else pltpu.roll(base, i, 1)
                if i < 2 * BAND or i >= nodes - 2 * BAND:
                    near = jnp.abs(row + i - lane) < nodes // 2
                    bell = jnp.where(near, bell, 0.0)
                bells.append(bell)
            for w in range(WEIGHTS):
                weight = np.float32(0.1) + np.float32(0.1) * np.float32(w)
                first = (k + w * SPREADS) * (OFFSETS * nodes) + o * nodes
                for i in range(0, len(bells), 2):
                    pair = jnp.concatenate([weight * bells[i], weight * bells[i + 1]], axis=0)
                    at = pl.ds(pl.multiple_of(first + i * 8, ROW), ROW)
                    tab_ref[at, :] = pair.astype(jnp.bfloat16)
        return carry

    lax.fori_loop(0, SPREADS, one, 0)


def fill_codes(dims, counts, owner_ref, target_ref, source_ref, seed_ref, codes_ref):
    events, comps, eblocks, nodes = dims["field"]
    half, subs, blocks = dims["half"], dims["subs"], dims["blocks"]
    groups = dims["tiles"] // LANES
    lists = events * groups
    me = lax.axis_index("mesh")
    lane = lax.broadcasted_iota(jnp.int32, (1, LANES), 1)
    for v in range(events):
        for g in range(groups):
            at = pl.ds(g * LANES, LANES)
            live = lane + g * LANES < counts[v]
            r = owner_ref[v, :, at] ^ me
            slot = ((r & 1) * half + (r >> 1)) * subs + target_ref[pl.ds(v, 1), at]
            source = source_ref[pl.ds(v, 1), at] + v * eblocks
            seed = seed_ref[pl.ds(v, 1), at]
            turned = 2 * OFFSETS * ((seed * 9363) >> 16) - seed + (OFFSETS - 1)
            codes = (
                jnp.where(live, source, events * eblocks) * PITCH,
                jnp.where(live, slot, blocks) * comps,
                seed * nodes,
                turned * nodes,
            )
            for n, code in enumerate(codes):
                codes_ref[pl.ds(n * lists + v * groups + g, 1), :] = code


def tile_loop(v, count, groups, load, add):
    def group(i, carry):
        results = []
        for u in range(0, LANES, 2):
            x0, g0 = load(v * groups + i, u)
            x1, g1 = load(v * groups + i, u + 1)
            y = jnp.dot(
                jnp.concatenate([x0, x1], axis=0),
                jnp.concatenate([g0, g1], axis=1),
                preferred_element_type=jnp.float32,
            )
            results += [y[:ROW, :LANES], y[ROW:, LANES:]]
        for u in range(LANES):
            add(v * groups + i, u, results[u])
        return carry

    lax.fori_loop(0, (count + LANES - 1) // LANES, group, 0)


def forward_kernel(
    dims, count_hbm, owner_hbm, target_hbm, source_hbm, seed_hbm, field_hbm, order_ref,
    sum_ref, tab_ref, codes_ref,
    raw_ref, rows_ref, owner_ref, target_ref, source_ref, seed_ref, count_ref, code_ref, sems,
):
    events, comps, eblocks, nodes = dims["field"]
    groups = dims["tiles"] // LANES
    lists = events * groups
    pairs = (
        (count_hbm, count_ref), (owner_hbm, owner_ref), (target_hbm, target_ref),
        (source_hbm, source_ref), (seed_hbm, seed_ref), (field_hbm, raw_ref),
    )
    fetches = [pltpu.make_async_copy(a, b, sems.at[n]) for n, (a, b) in enumerate(pairs)]
    for fetch in fetches:
        fetch.start()
    sum_ref[...] = jnp.zeros_like(sum_ref)
    for fetch in fetches[:-1]:
        fetch.wait()
    counts = [count_ref[0, v] for v in range(events)]
    fill_codes(dims, counts, owner_ref, target_ref, source_ref, seed_ref, codes_ref)
    fill_table(tab_ref, nodes)
    to_smem = pltpu.make_async_copy(codes_ref, code_ref, sems.at[len(pairs)])
    to_smem.start()
    fetches[-1].wait()
    for v in range(events):
        for c in range(comps):
            rows_ref[pl.ds(v * eblocks * PITCH + c, eblocks, stride=PITCH), :] = raw_ref[
                v, c
            ].astype(jnp.float32)
    to_smem.wait()

    def load(i, u):
        shape = pl.multiple_of(code_ref[2 * lists + i, u], nodes)
        x = rows_ref[pl.ds(code_ref[i, u], ROW), :]
        return x.astype(jnp.bfloat16), tab_ref[pl.ds(shape, nodes), :]

    def add(i, u, y):
        at = pl.ds(pl.multiple_of(code_ref[lists + i, u], 4), comps)
        y = y.astype(jnp.bfloat16).astype(jnp.float32)
        sum_ref[at, :] = sum_ref[at, :] + y[:comps]

    for v in range(events):
        tile_loop(v, counts[v], groups, load, add)


def backward_kernel(dims, count_ref, codes_in, tab_ref, *refs):
    events, comps, eblocks, nodes = dims["field"]
    half, subs = dims["half"], dims["subs"]
    groups = dims["tiles"] // LANES
    lists = events * groups
    mine_refs, (other_ref, out_ref, rows_ref, sum_ref, tile_ref, code_ref, sems) = (
        refs[:half], refs[half:],
    )
    to_smem = pltpu.make_async_copy(codes_in, code_ref, sems.at[0])
    to_smem.start()
    sum_ref[...] = jnp.zeros_like(sum_ref)
    part = subs * comps
    for j in range(half):
        rows_ref[pl.ds(j * part, part), :] = mine_refs[j][...].astype(jnp.float32)
        rows_ref[pl.ds((half + j) * part, part), :] = other_ref[j].astype(jnp.float32)
    to_smem.wait()

    def load(i, u):
        shape = pl.multiple_of(code_ref[3 * lists + i, u], nodes)
        x = rows_ref[pl.ds(pl.multiple_of(code_ref[lists + i, u], 4), ROW), :]
        return x.astype(jnp.bfloat16), tab_ref[pl.ds(shape, nodes), :]

    def add(i, u, y):
        at = pl.ds(code_ref[i, u], comps)
        sum_ref[at, :] = sum_ref[at, :] + y[:comps]

    sends = []
    for v in range(events):
        tile_loop(v, count_ref[0, v], groups, load, add)
        for c in range(comps):
            tile_ref[v, c] = sum_ref[pl.ds(v * eblocks * PITCH + c, eblocks, stride=PITCH), :]
        send = pltpu.make_async_copy(tile_ref.at[v], out_ref.at[v], sems.at[1 + v])
        send.start()
        sends.append(send)
    for send in sends:
        send.wait()


def pack_kernel(comps, group, *refs):
    ins, (out_ref, wide_ref) = refs[:-2], refs[-2:]
    rows = comps * group
    for n, ref in enumerate(ins):
        for c in range(comps):
            wide_ref[pl.ds(c, group, stride=PITCH), :] = ref[c, 0]
        for s in range(group):
            out_ref[n, pl.ds(s * comps, comps), :] = wide_ref[pl.ds(s * PITCH, comps), :]


def terms(a_ref, b_ref, hist_ref, k, rows, evs):
    group = lax.axis_index("ev") ^ k
    at = pl.ds(pl.multiple_of(group * rows, 8), rows)
    gradient = a_ref[at, :] + b_ref[at, :]
    prev_gradient, prev_step, precond = hist_ref[k, 0], hist_ref[k, 1], hist_ref[k, 2]
    return at, gradient, gradient - prev_gradient, prev_step, precond


def sums_kernel(rows, evs, a_ref, b_ref, hist_ref, out_ref):
    total = [jnp.zeros((8, LANES), jnp.float32) for _ in range(4)]
    for k in range(evs):
        _, gradient, change, prev_step, precond = terms(a_ref, b_ref, hist_ref, k, rows, evs)
        weighted = precond * change
        parts = (prev_step * change, prev_step * gradient, weighted * gradient, weighted * change)
        for n, part in enumerate(parts):
            total[n] = total[n] + jnp.sum(part.reshape(rows // 8, 8, LANES), axis=0)
    for n in range(4):
        out_ref[pl.ds(n, 1), :] = jnp.sum(total[n], axis=0, keepdims=True)
    out_ref[pl.ds(4, 4), :] = jnp.zeros((4, LANES), jnp.float32)


def direction_kernel(rows, evs, comps, group, a_ref, b_ref, hist_ref, *refs):
    sum_refs, (inv_ref, round_ref, wide_ref) = refs[:-3], refs[-3:]
    level = [ref[...] for ref in sum_refs]
    while len(level) > 1:
        level = [level[i] + level[i + 1] for i in range(0, len(level), 2)]
    sums = jnp.sum(level[0], axis=1, keepdims=True)
    curvature, slope, cross_term, self_term = (sums[n : n + 1] for n in range(4))
    alpha = slope / curvature
    beta = (cross_term - alpha * self_term) / curvature
    bend = alpha - beta
    for k in range(evs):
        at, gradient, change, prev_step, precond = terms(a_ref, b_ref, hist_ref, k, rows, evs)
        scaled = precond * (gradient - alpha * change)
        direction = -(scaled + bend * prev_step)
        round_ref[at, :] = direction.astype(jnp.bfloat16)
        if k == 0:
            for s in range(group):
                wide_ref[pl.ds(s * PITCH, comps), :] = direction[s * comps : (s + 1) * comps]
            for c in range(comps):
                inv_ref[c, 0] = wide_ref[pl.ds(c, group, stride=PITCH), :]


def in_smem():
    return pl.BlockSpec(memory_space=pltpu.SMEM)


def in_vmem():
    return pl.BlockSpec(memory_space=pltpu.VMEM)


def in_hbm():
    return pl.BlockSpec(memory_space=pltpu.HBM)


def limit(mib):
    return pltpu.CompilerParams(vmem_limit_bytes=mib << 20)


def f32(*shape):
    return jax.ShapeDtypeStruct(shape, jnp.float32)


def bf16(*shape):
    return jax.ShapeDtypeStruct(shape, jnp.bfloat16)


def body(
    kernels, tile_owner, tile_source, tile_target, tile_seed, tile_count, prev_gradient,
    prev_step, precond,
):
    events, comps, eblocks, nodes = kernels.shape
    parts = lax.axis_size("mesh")
    evs = lax.axis_size("ev")
    group = precond.shape[2]
    subs = group * evs
    blocks = parts * subs
    half = parts // 2
    rows = comps * group
    part_rows = comps * subs
    tiles = tile_source.shape[1]
    dims = dict(field=kernels.shape, half=half, subs=subs, blocks=blocks, tiles=tiles)

    def swap(x, axis, k):
        size = parts if axis == "mesh" else evs
        return lax.ppermute(x, axis, [(i, i ^ k) for i in range(size)])

    owners = jnp.transpose(tile_owner, (0, 2, 1))
    counts = jnp.transpose(tile_count)
    table = bf16(SHAPES * nodes, nodes)
    code_rows = (CODES * events * tiles // LANES, LANES)
    codes_shape = jax.ShapeDtypeStruct(code_rows, jnp.int32)

    packed = pl.pallas_call(
        functools.partial(pack_kernel, comps, group),
        out_shape=f32(3, rows, nodes),
        in_specs=[in_vmem()] * 3,
        out_specs=in_vmem(),
        scratch_shapes=[pltpu.VMEM((group * PITCH, nodes), jnp.float32)],
        compiler_params=limit(2),
        name="pack",
    )(prev_gradient, prev_step, precond)
    hist = jnp.stack([packed] + [swap(packed, "ev", k) for k in range(1, evs)])

    sums, tab, codes = pl.pallas_call(
        functools.partial(forward_kernel, dims),
        out_shape=[f32(blocks * comps + ROW, nodes), table, codes_shape],
        in_specs=[in_hbm()] * 6 + [in_vmem()],
        out_specs=[in_vmem()] * 3,
        scratch_shapes=[
            pltpu.VMEM(kernels.shape, jnp.bfloat16),
            pltpu.VMEM((events * eblocks * PITCH + ROW, nodes), jnp.float32),
            pltpu.VMEM(owners.shape, jnp.int32),
            pltpu.VMEM(tile_target.shape, jnp.int32),
            pltpu.VMEM(tile_source.shape, jnp.int32),
            pltpu.VMEM(tile_seed.shape, jnp.int32),
            pltpu.SMEM(counts.shape, jnp.int32),
            pltpu.SMEM(code_rows, jnp.int32),
            pltpu.SemaphoreType.DMA((7,)),
        ],
        compiler_params=limit(20),
        cost_estimate=pl.CostEstimate(
            flops=2 * events * tiles * ROW * nodes * nodes * 64,
            bytes_accessed=16 << 20,
            transcendentals=0,
        ),
        name="forward",
    )(counts, owners, tile_target, tile_source, tile_seed, kernels, packed)

    keep = sums[: half * part_rows].reshape(half, part_rows, nodes)
    send = sums[half * part_rows : 2 * half * part_rows].reshape(half, part_rows, nodes)
    got = swap(send, "mesh", 1)
    held = [keep[j] + got[j] for j in range(half)]
    arrived = [swap(held[j], "mesh", 2 * j) for j in range(1, half)]
    total = held[0]
    for piece in arrived:
        total = total + piece
    bits = evs.bit_length() - 1
    for bit in range(bits - 1):
        total = total + swap(total, "ev", 1 << bit)
    across = swap(total, "ev", 1 << (bits - 1))

    local = pl.pallas_call(
        functools.partial(sums_kernel, rows, evs),
        out_shape=f32(8, nodes),
        in_specs=[in_vmem()] * 3,
        out_specs=in_vmem(),
        compiler_params=limit(4),
        name="sums",
    )(total, across, hist)
    local = local + swap(local, "mesh", 1)
    spread = [local] + [swap(local, "mesh", 2 * j) for j in range(1, half)]
    inversion_direction, rounded = pl.pallas_call(
        functools.partial(direction_kernel, rows, evs, comps, group),
        out_shape=[f32(*precond.shape), bf16(part_rows, nodes)],
        in_specs=[in_vmem()] * (3 + half),
        out_specs=[in_vmem()] * 2,
        scratch_shapes=[pltpu.VMEM((group * PITCH, nodes), jnp.float32)],
        compiler_params=limit(4),
        name="direction",
    )(total, across, hist, *spread)

    mine = [rounded] + [swap(rounded, "mesh", 2 * j) for j in range(1, half)]
    other = swap(jnp.stack(mine), "mesh", 1)

    event_direction = pl.pallas_call(
        functools.partial(backward_kernel, dims),
        out_shape=f32(*kernels.shape),
        in_specs=[in_smem()] + [in_vmem()] * (half + 3),
        out_specs=in_hbm(),
        scratch_shapes=[
            pltpu.VMEM((blocks * comps + ROW, nodes), jnp.float32),
            pltpu.VMEM((events * eblocks * PITCH + ROW, nodes), jnp.float32),
            pltpu.VMEM(kernels.shape, jnp.float32),
            pltpu.SMEM(code_rows, jnp.int32),
            pltpu.SemaphoreType.DMA((1 + events,)),
        ],
        compiler_params=limit(24),
        name="backward",
    )(counts, codes, tab, *mine, other)
    return inversion_direction, event_direction


def solution(mesh):
    in_specs = (
        P("ev", None, "mesh", None),
        P("ev", "mesh", None),
        P("ev", "mesh"),
        P("ev", "mesh"),
        P("ev", "mesh"),
        P("ev", "mesh"),
        P(None, "mesh", "ev", None),
        P(None, "mesh", "ev", None),
        P(None, "mesh", "ev", None),
    )
    out_specs = (P(None, "mesh", "ev", None), P("ev", None, "mesh", None))
    return jax.shard_map(body, mesh=mesh, in_specs=in_specs, out_specs=out_specs, check_vma=False)
```

```python
import functools

import jax
import jax.numpy as jnp
import numpy as np
from jax import lax
from jax.experimental import pallas as pl
from jax.experimental.pallas import tpu as pltpu
from jax.sharding import PartitionSpec as P


OFFSETS = 7
SPREADS = 3
WEIGHTS = 4
SHAPES = OFFSETS * SPREADS * WEIGHTS
ROW = 16
PITCH = 13
LANES = 128
BAND = 16
CODES = 4


def table_kernel(nodes, tab_ref):
    row = lax.broadcasted_iota(jnp.int32, (8, nodes), 0)
    lane = lax.broadcasted_iota(jnp.int32, (8, nodes), 1)
    signed = jnp.where(lane < nodes // 2, lane, lane - nodes)

    def one(k, carry):
        spread = 0.55 + 0.1 * k.astype(jnp.float32)
        for o in range(OFFSETS):
            distance = (row - signed - (o - OFFSETS // 2)).astype(jnp.float32)
            base = jnp.exp(-distance * distance / (2.0 * spread * spread))
            bells = []
            for i in range(0, nodes, 8):
                bell = base if i == 0 else pltpu.roll(base, i, 1)
                if i < 2 * BAND or i >= nodes - 2 * BAND:
                    near = jnp.abs(row + i - lane) < nodes // 2
                    bell = jnp.where(near, bell, 0.0)
                bells.append(bell)
            for w in range(WEIGHTS):
                weight = np.float32(0.1) + np.float32(0.1) * np.float32(w)
                first = (k + w * SPREADS) * (OFFSETS * nodes) + o * nodes
                for i in range(0, len(bells), 2):
                    pair = jnp.concatenate([weight * bells[i], weight * bells[i + 1]], axis=0)
                    at = pl.ds(pl.multiple_of(first + i * 8, ROW), ROW)
                    tab_ref[at, :] = pair.astype(jnp.bfloat16)
        return carry

    lax.fori_loop(0, SPREADS, one, 0)


def fill_codes(dims, counts, owner_ref, target_ref, source_ref, seed_ref, codes_ref):
    events, comps, eblocks, nodes = dims["field"]
    half, subs, blocks = dims["half"], dims["subs"], dims["blocks"]
    groups = dims["tiles"] // LANES
    lists = events * groups
    me = lax.axis_index("mesh")
    lane = lax.broadcasted_iota(jnp.int32, (1, LANES), 1)
    for v in range(events):
        for g in range(groups):
            at = pl.ds(g * LANES, LANES)
            live = lane + g * LANES < counts[v]
            r = owner_ref[v, :, at] ^ me
            slot = ((r & 1) * half + (r >> 1)) * subs + target_ref[pl.ds(v, 1), at]
            source = source_ref[pl.ds(v, 1), at] + v * eblocks
            seed = seed_ref[pl.ds(v, 1), at]
            turned = 2 * OFFSETS * ((seed * 9363) >> 16) - seed + (OFFSETS - 1)
            codes = (
                jnp.where(live, source, events * eblocks) * PITCH,
                jnp.where(live, slot, blocks) * comps,
                seed * nodes,
                turned * nodes,
            )
            for n, code in enumerate(codes):
                codes_ref[pl.ds(n * lists + v * groups + g, 1), :] = code


def tile_loop(v, count, groups, load, add):
    def group(i, carry):
        results = []
        for u in range(0, LANES, 2):
            x0, g0 = load(v * groups + i, u)
            x1, g1 = load(v * groups + i, u + 1)
            y = jnp.dot(
                jnp.concatenate([x0, x1], axis=0),
                jnp.concatenate([g0, g1], axis=1),
                preferred_element_type=jnp.float32,
            )
            results += [y[:ROW, :LANES], y[ROW:, LANES:]]
        for u in range(LANES):
            add(v * groups + i, u, results[u])
        return carry

    lax.fori_loop(0, (count + LANES - 1) // LANES, group, 0)


def forward_kernel(
    dims, count_ref, owner_ref, target_ref, source_ref, seed_ref, field_ref, tab_ref,
    sum_ref, codes_ref, rows_ref, code_ref, sems,
):
    events, comps, eblocks, nodes = dims["field"]
    groups = dims["tiles"] // LANES
    lists = events * groups
    counts = [count_ref[0, v] for v in range(events)]
    fill_codes(dims, counts, owner_ref, target_ref, source_ref, seed_ref, codes_ref)
    sum_ref[...] = jnp.zeros_like(sum_ref)
    to_smem = pltpu.make_async_copy(codes_ref, code_ref, sems.at[0])
    to_smem.start()
    for v in range(events):
        for c in range(comps):
            rows_ref[pl.ds(v * eblocks * PITCH + c, eblocks, stride=PITCH), :] = field_ref[
                v, c
            ].astype(jnp.float32)
    to_smem.wait()

    def load(i, u):
        shape = pl.multiple_of(code_ref[2 * lists + i, u], nodes)
        x = rows_ref[pl.ds(code_ref[i, u], ROW), :]
        return x.astype(jnp.bfloat16), tab_ref[pl.ds(shape, nodes), :]

    def add(i, u, y):
        at = pl.ds(pl.multiple_of(code_ref[lists + i, u], 4), comps)
        y = y.astype(jnp.bfloat16).astype(jnp.float32)
        sum_ref[at, :] = sum_ref[at, :] + y[:comps]

    for v in range(events):
        tile_loop(v, counts[v], groups, load, add)


def backward_kernel(dims, count_ref, codes_in, tab_ref, *refs):
    events, comps, eblocks, nodes = dims["field"]
    half, subs = dims["half"], dims["subs"]
    groups = dims["tiles"] // LANES
    lists = events * groups
    mine_refs, (other_ref, out_ref, rows_ref, sum_ref, tile_ref, code_ref, sems) = (
        refs[:half], refs[half:],
    )
    to_smem = pltpu.make_async_copy(codes_in, code_ref, sems.at[0])
    to_smem.start()
    sum_ref[...] = jnp.zeros_like(sum_ref)
    part = subs * comps
    for j in range(half):
        rows_ref[pl.ds(j * part, part), :] = mine_refs[j][...].astype(jnp.float32)
        rows_ref[pl.ds((half + j) * part, part), :] = other_ref[j].astype(jnp.float32)
    to_smem.wait()

    def load(i, u):
        shape = pl.multiple_of(code_ref[3 * lists + i, u], nodes)
        x = rows_ref[pl.ds(pl.multiple_of(code_ref[lists + i, u], 4), ROW), :]
        return x.astype(jnp.bfloat16), tab_ref[pl.ds(shape, nodes), :]

    def add(i, u, y):
        at = pl.ds(code_ref[i, u], comps)
        sum_ref[at, :] = sum_ref[at, :] + y[:comps]

    sends = []
    for v in range(events):
        tile_loop(v, count_ref[0, v], groups, load, add)
        for c in range(comps):
            tile_ref[v, c] = sum_ref[pl.ds(v * eblocks * PITCH + c, eblocks, stride=PITCH), :]
        send = pltpu.make_async_copy(tile_ref.at[v], out_ref.at[v], sems.at[1 + v])
        send.start()
        sends.append(send)
    for send in sends:
        send.wait()


def pack_kernel(comps, group, *refs):
    ins, (out_ref, wide_ref) = refs[:-2], refs[-2:]
    for n, ref in enumerate(ins):
        for c in range(comps):
            wide_ref[pl.ds(c, group, stride=PITCH), :] = ref[c, 0]
        for s in range(group):
            out_ref[n, pl.ds(s * comps, comps), :] = wide_ref[pl.ds(s * PITCH, comps), :]


def fold_kernel(a_ref, b_ref, out_ref):
    out_ref[...] = a_ref[...] + b_ref[...]


def terms(a_ref, b_ref, hist_ref, k, rows):
    group = lax.axis_index("ev") ^ k
    at = pl.ds(pl.multiple_of(group * rows, 8), rows)
    gradient = a_ref[at, :] + b_ref[at, :]
    prev_gradient, prev_step, precond = hist_ref[k, 0], hist_ref[k, 1], hist_ref[k, 2]
    return at, gradient, gradient - prev_gradient, prev_step, precond


def sums_kernel(rows, evs, a_ref, b_ref, hist_ref, out_ref):
    total = [jnp.zeros((8, LANES), jnp.float32) for _ in range(4)]
    for k in range(evs):
        _, gradient, change, prev_step, precond = terms(a_ref, b_ref, hist_ref, k, rows)
        weighted = precond * change
        parts = (prev_step * change, prev_step * gradient, weighted * gradient, weighted * change)
        for n, part in enumerate(parts):
            total[n] = total[n] + jnp.sum(part.reshape(rows // 8, 8, LANES), axis=0)
    for n in range(4):
        out_ref[pl.ds(n, 1), :] = jnp.sum(total[n], axis=0, keepdims=True)
    out_ref[pl.ds(4, 4), :] = jnp.zeros((4, LANES), jnp.float32)


def direction_kernel(rows, evs, comps, group, a_ref, b_ref, hist_ref, *refs):
    sum_refs, (inv_ref, round_ref, wide_ref) = refs[:-3], refs[-3:]
    level = [ref[...] for ref in sum_refs]
    while len(level) > 1:
        level = [level[i] + level[i + 1] for i in range(0, len(level), 2)]
    sums = jnp.sum(level[0], axis=1, keepdims=True)
    curvature, slope, cross_term, self_term = (sums[n : n + 1] for n in range(4))
    alpha = slope / curvature
    beta = (cross_term - alpha * self_term) / curvature
    bend = alpha - beta
    for k in range(evs):
        at, gradient, change, prev_step, precond = terms(a_ref, b_ref, hist_ref, k, rows)
        scaled = precond * (gradient - alpha * change)
        direction = -(scaled + bend * prev_step)
        round_ref[at, :] = direction.astype(jnp.bfloat16)
        if k == 0:
            for s in range(group):
                wide_ref[pl.ds(s * PITCH, comps), :] = direction[s * comps : (s + 1) * comps]
            for c in range(comps):
                inv_ref[c, 0] = wide_ref[pl.ds(c, group, stride=PITCH), :]


def in_smem():
    return pl.BlockSpec(memory_space=pltpu.SMEM)


def in_vmem():
    return pl.BlockSpec(memory_space=pltpu.VMEM)


def in_hbm():
    return pl.BlockSpec(memory_space=pltpu.HBM)


def limit(mib):
    return pltpu.CompilerParams(vmem_limit_bytes=mib << 20)


def f32(*shape):
    return jax.ShapeDtypeStruct(shape, jnp.float32)


def bf16(*shape):
    return jax.ShapeDtypeStruct(shape, jnp.bfloat16)


def body(
    kernels, tile_owner, tile_source, tile_target, tile_seed, tile_count, prev_gradient,
    prev_step, precond,
):
    events, comps, eblocks, nodes = kernels.shape
    parts = lax.axis_size("mesh")
    evs = lax.axis_size("ev")
    group = precond.shape[2]
    subs = group * evs
    blocks = parts * subs
    half = parts // 2
    rows = comps * group
    part_rows = comps * subs
    tiles = tile_source.shape[1]
    dims = dict(field=kernels.shape, half=half, subs=subs, blocks=blocks, tiles=tiles)

    def swap(x, axis, k):
        size = parts if axis == "mesh" else evs
        return lax.ppermute(x, axis, [(i, i ^ k) for i in range(size)])

    owners = jnp.transpose(tile_owner, (0, 2, 1))
    counts = jnp.transpose(tile_count)
    table = bf16(SHAPES * nodes, nodes)
    code_rows = (CODES * events * tiles // LANES, LANES)
    codes_shape = jax.ShapeDtypeStruct(code_rows, jnp.int32)

    packed = pl.pallas_call(
        functools.partial(pack_kernel, comps, group),
        out_shape=f32(3, rows, nodes),
        in_specs=[in_vmem()] * 3,
        out_specs=in_vmem(),
        scratch_shapes=[pltpu.VMEM((group * PITCH, nodes), jnp.float32)],
        compiler_params=limit(2),
        name="pack",
    )(prev_gradient, prev_step, precond)
    hist = [packed]
    for k in range(1, evs):
        hist.append(swap(packed, "ev", k))
    hist = jnp.stack(hist)

    tab = pl.pallas_call(
        functools.partial(table_kernel, nodes),
        out_shape=table,
        out_specs=in_vmem(),
        compiler_params=limit(1),
        cost_estimate=pl.CostEstimate(flops=1 << 28, bytes_accessed=4 << 20, transcendentals=0),
        name="table",
    )()
    sums, codes = pl.pallas_call(
        functools.partial(forward_kernel, dims),
        out_shape=[f32(blocks * comps + ROW, nodes), codes_shape],
        in_specs=[in_smem()] + [in_vmem()] * 6,
        out_specs=[in_vmem()] * 2,
        scratch_shapes=[
            pltpu.VMEM((events * eblocks * PITCH + ROW, nodes), jnp.float32),
            pltpu.SMEM(code_rows, jnp.int32),
            pltpu.SemaphoreType.DMA((1,)),
        ],
        compiler_params=limit(20),
        cost_estimate=pl.CostEstimate(
            flops=2 * events * tiles * ROW * nodes * nodes * 64,
            bytes_accessed=16 << 20,
            transcendentals=0,
        ),
        name="forward",
    )(counts, owners, tile_target, tile_source, tile_seed, kernels, tab)

    keep = sums[: half * part_rows].reshape(half, part_rows, nodes)
    send = sums[half * part_rows : 2 * half * part_rows].reshape(half, part_rows, nodes)
    got = swap(send, "mesh", 1)
    held = [None] + [keep[j] + got[j] for j in range(1, half)]
    arrived = []
    for j in range(1, half):
        arrived.append(swap(held[j], "mesh", 2 * j))
    total = pl.pallas_call(
        fold_kernel,
        out_shape=f32(part_rows, nodes),
        in_specs=[in_vmem()] * 2,
        out_specs=in_vmem(),
        compiler_params=limit(2),
        name="fold",
    )(keep[0], got[0])
    for piece in arrived:
        total = total + piece
    bits = evs.bit_length() - 1
    for bit in range(bits - 1):
        total = total + swap(total, "ev", 1 << bit)
    across = swap(total, "ev", 1 << (bits - 1))

    local = pl.pallas_call(
        functools.partial(sums_kernel, rows, evs),
        out_shape=f32(8, nodes),
        in_specs=[in_vmem()] * 3,
        out_specs=in_vmem(),
        compiler_params=limit(4),
        name="sums",
    )(total, across, hist)
    local = local + swap(local, "mesh", 1)
    spread = [local] + [swap(local, "mesh", 2 * j) for j in range(1, half)]
    inversion_direction, rounded = pl.pallas_call(
        functools.partial(direction_kernel, rows, evs, comps, group),
        out_shape=[f32(*precond.shape), bf16(part_rows, nodes)],
        in_specs=[in_vmem()] * (3 + half),
        out_specs=[in_vmem()] * 2,
        scratch_shapes=[pltpu.VMEM((group * PITCH, nodes), jnp.float32)],
        compiler_params=limit(4),
        name="direction",
    )(total, across, hist, *spread)

    mine = [rounded] + [swap(rounded, "mesh", 2 * j) for j in range(1, half)]
    other = swap(jnp.stack(mine), "mesh", 1)

    event_direction = pl.pallas_call(
        functools.partial(backward_kernel, dims),
        out_shape=f32(*kernels.shape),
        in_specs=[in_smem()] + [in_vmem()] * (half + 3),
        out_specs=in_hbm(),
        scratch_shapes=[
            pltpu.VMEM((blocks * comps + ROW, nodes), jnp.float32),
            pltpu.VMEM((events * eblocks * PITCH + ROW, nodes), jnp.float32),
            pltpu.VMEM(kernels.shape, jnp.float32),
            pltpu.SMEM(code_rows, jnp.int32),
            pltpu.SemaphoreType.DMA((1 + events,)),
        ],
        compiler_params=limit(24),
        name="backward",
    )(counts, codes, tab, *mine, other)
    return inversion_direction, event_direction


def solution(mesh):
    in_specs = (
        P("ev", None, "mesh", None),
        P("ev", "mesh", None),
        P("ev", "mesh"),
        P("ev", "mesh"),
        P("ev", "mesh"),
        P("ev", "mesh"),
        P(None, "mesh", "ev", None),
        P(None, "mesh", "ev", None),
        P(None, "mesh", "ev", None),
    )
    out_specs = (P(None, "mesh", "ev", None), P("ev", None, "mesh", None))

    return jax.shard_map(body, mesh=mesh, in_specs=in_specs, out_specs=out_specs, check_vma=False)
```

```python
import functools

import jax
import jax.numpy as jnp
import numpy as np
from jax import lax
from jax.experimental import pallas as pl
from jax.experimental.pallas import tpu as pltpu
from jax.sharding import PartitionSpec as P


OFFSETS = 7
SPREADS = 3
WEIGHTS = 4
SHAPES = OFFSETS * SPREADS * WEIGHTS
ROW = 16
PITCH = 13
LANES = 128
BAND = 16
CODES = 4


def table_kernel(nodes, tab_ref):
    row = lax.broadcasted_iota(jnp.int32, (8, nodes), 0)
    lane = lax.broadcasted_iota(jnp.int32, (8, nodes), 1)
    signed = jnp.where(lane < nodes // 2, lane, lane - nodes)

    def one(k, carry):
        spread = 0.55 + 0.1 * k.astype(jnp.float32)
        for o in range(OFFSETS):
            distance = (row - signed - (o - OFFSETS // 2)).astype(jnp.float32)
            base = jnp.exp(-distance * distance / (2.0 * spread * spread))
            bells = []
            for i in range(0, nodes, 8):
                bell = base if i == 0 else pltpu.roll(base, i, 1)
                if i < 2 * BAND or i >= nodes - 2 * BAND:
                    near = jnp.abs(row + i - lane) < nodes // 2
                    bell = jnp.where(near, bell, 0.0)
                bells.append(bell)
            for w in range(WEIGHTS):
                weight = np.float32(0.1) + np.float32(0.1) * np.float32(w)
                first = (k + w * SPREADS) * (OFFSETS * nodes) + o * nodes
                for i in range(0, len(bells), 2):
                    pair = jnp.concatenate([weight * bells[i], weight * bells[i + 1]], axis=0)
                    at = pl.ds(pl.multiple_of(first + i * 8, ROW), ROW)
                    tab_ref[at, :] = pair.astype(jnp.bfloat16)
        return carry

    lax.fori_loop(0, SPREADS, one, 0)


def fill_codes(dims, counts, owner_ref, target_ref, source_ref, seed_ref, codes_ref):
    events, comps, eblocks, nodes = dims["field"]
    half, subs, blocks = dims["half"], dims["subs"], dims["blocks"]
    groups = dims["tiles"] // LANES
    lists = events * groups
    me = lax.axis_index("mesh")
    lane = lax.broadcasted_iota(jnp.int32, (1, LANES), 1)
    for v in range(events):
        for g in range(groups):
            at = pl.ds(g * LANES, LANES)
            live = lane + g * LANES < counts[v]
            r = owner_ref[v, :, at] ^ me
            slot = ((r & 1) * half + (r >> 1)) * subs + target_ref[pl.ds(v, 1), at]
            source = source_ref[pl.ds(v, 1), at] + v * eblocks
            seed = seed_ref[pl.ds(v, 1), at]
            turned = 2 * OFFSETS * ((seed * 9363) >> 16) - seed + (OFFSETS - 1)
            codes = (
                jnp.where(live, source, events * eblocks) * PITCH,
                jnp.where(live, slot, blocks) * comps,
                seed * nodes,
                turned * nodes,
            )
            for n, code in enumerate(codes):
                codes_ref[pl.ds(n * lists + v * groups + g, 1), :] = code


def tile_loop(v, count, groups, load, add):
    def group(i, carry):
        results = []
        for u in range(0, LANES, 2):
            x0, g0 = load(v * groups + i, u)
            x1, g1 = load(v * groups + i, u + 1)
            y = jnp.dot(
                jnp.concatenate([x0, x1], axis=0),
                jnp.concatenate([g0, g1], axis=1),
                preferred_element_type=jnp.float32,
            )
            results += [y[:ROW, :LANES], y[ROW:, LANES:]]
        for u in range(LANES):
            add(v * groups + i, u, results[u])
        return carry

    lax.fori_loop(0, (count + LANES - 1) // LANES, group, 0)


def forward_kernel(
    dims, count_ref, owner_ref, target_ref, source_ref, seed_ref, field_ref, tab_ref,
    sum_ref, codes_ref, rows_ref, code_ref, sems,
):
    events, comps, eblocks, nodes = dims["field"]
    groups = dims["tiles"] // LANES
    lists = events * groups
    counts = [count_ref[0, v] for v in range(events)]
    fill_codes(dims, counts, owner_ref, target_ref, source_ref, seed_ref, codes_ref)
    sum_ref[...] = jnp.zeros_like(sum_ref)
    to_smem = pltpu.make_async_copy(codes_ref, code_ref, sems.at[0])
    to_smem.start()
    for v in range(events):
        for c in range(comps):
            rows_ref[pl.ds(v * eblocks * PITCH + c, eblocks, stride=PITCH), :] = field_ref[
                v, c
            ].astype(jnp.float32)
    to_smem.wait()

    def load(i, u):
        shape = pl.multiple_of(code_ref[2 * lists + i, u], nodes)
        x = rows_ref[pl.ds(code_ref[i, u], ROW), :]
        return x.astype(jnp.bfloat16), tab_ref[pl.ds(shape, nodes), :]

    def add(i, u, y):
        at = pl.ds(pl.multiple_of(code_ref[lists + i, u], 4), comps)
        y = y.astype(jnp.bfloat16).astype(jnp.float32)
        sum_ref[at, :] = sum_ref[at, :] + y[:comps]

    for v in range(events):
        tile_loop(v, counts[v], groups, load, add)


def backward_kernel(dims, count_ref, codes_in, tab_ref, *refs):
    events, comps, eblocks, nodes = dims["field"]
    half, subs = dims["half"], dims["subs"]
    groups = dims["tiles"] // LANES
    lists = events * groups
    mine_refs, (other_ref, out_ref, rows_ref, sum_ref, tile_ref, code_ref, sems) = (
        refs[:half], refs[half:],
    )
    to_smem = pltpu.make_async_copy(codes_in, code_ref, sems.at[0])
    to_smem.start()
    sum_ref[...] = jnp.zeros_like(sum_ref)
    part = subs * comps
    for j in range(half):
        rows_ref[pl.ds(j * part, part), :] = mine_refs[j][...].astype(jnp.float32)
        rows_ref[pl.ds((half + j) * part, part), :] = other_ref[j].astype(jnp.float32)
    to_smem.wait()

    def load(i, u):
        shape = pl.multiple_of(code_ref[3 * lists + i, u], nodes)
        x = rows_ref[pl.ds(pl.multiple_of(code_ref[lists + i, u], 4), ROW), :]
        return x.astype(jnp.bfloat16), tab_ref[pl.ds(shape, nodes), :]

    def add(i, u, y):
        at = pl.ds(code_ref[i, u], comps)
        sum_ref[at, :] = sum_ref[at, :] + y[:comps]

    sends = []
    for v in range(events):
        tile_loop(v, count_ref[0, v], groups, load, add)
        for c in range(comps):
            tile_ref[v, c] = sum_ref[pl.ds(v * eblocks * PITCH + c, eblocks, stride=PITCH), :]
        send = pltpu.make_async_copy(tile_ref.at[v], out_ref.at[v], sems.at[1 + v])
        send.start()
        sends.append(send)
    for send in sends:
        send.wait()


def pack_kernel(comps, group, *refs):
    ins, (out_ref, wide_ref) = refs[:-2], refs[-2:]
    for n, ref in enumerate(ins):
        for c in range(comps):
            wide_ref[pl.ds(c, group, stride=PITCH), :] = ref[c, 0]
        for s in range(group):
            out_ref[n, pl.ds(s * comps, comps), :] = wide_ref[pl.ds(s * PITCH, comps), :]


def terms(a_ref, b_ref, hist_ref, k, rows):
    group = lax.axis_index("ev") ^ k
    at = pl.ds(pl.multiple_of(group * rows, 8), rows)
    gradient = a_ref[at, :] + b_ref[at, :]
    prev_gradient, prev_step, precond = hist_ref[k, 0], hist_ref[k, 1], hist_ref[k, 2]
    return at, gradient, gradient - prev_gradient, prev_step, precond


def sums_kernel(rows, evs, a_ref, b_ref, hist_ref, out_ref):
    total = [jnp.zeros((8, LANES), jnp.float32) for _ in range(4)]
    for k in range(evs):
        _, gradient, change, prev_step, precond = terms(a_ref, b_ref, hist_ref, k, rows)
        weighted = precond * change
        parts = (prev_step * change, prev_step * gradient, weighted * gradient, weighted * change)
        for n, part in enumerate(parts):
            total[n] = total[n] + jnp.sum(part.reshape(rows // 8, 8, LANES), axis=0)
    for n in range(4):
        out_ref[pl.ds(n, 1), :] = jnp.sum(total[n], axis=0, keepdims=True)
    out_ref[pl.ds(4, 4), :] = jnp.zeros((4, LANES), jnp.float32)


def direction_kernel(rows, evs, comps, group, a_ref, b_ref, hist_ref, *refs):
    sum_refs, (inv_ref, round_ref, wide_ref) = refs[:-3], refs[-3:]
    level = [ref[...] for ref in sum_refs]
    while len(level) > 1:
        level = [level[i] + level[i + 1] for i in range(0, len(level), 2)]
    sums = jnp.sum(level[0], axis=1, keepdims=True)
    curvature, slope, cross_term, self_term = (sums[n : n + 1] for n in range(4))
    alpha = slope / curvature
    beta = (cross_term - alpha * self_term) / curvature
    bend = alpha - beta
    for k in range(evs):
        at, gradient, change, prev_step, precond = terms(a_ref, b_ref, hist_ref, k, rows)
        scaled = precond * (gradient - alpha * change)
        direction = -(scaled + bend * prev_step)
        round_ref[at, :] = direction.astype(jnp.bfloat16)
        if k == 0:
            for s in range(group):
                wide_ref[pl.ds(s * PITCH, comps), :] = direction[s * comps : (s + 1) * comps]
            for c in range(comps):
                inv_ref[c, 0] = wide_ref[pl.ds(c, group, stride=PITCH), :]


def in_smem():
    return pl.BlockSpec(memory_space=pltpu.SMEM)


def in_vmem():
    return pl.BlockSpec(memory_space=pltpu.VMEM)


def in_hbm():
    return pl.BlockSpec(memory_space=pltpu.HBM)


def limit(mib):
    return pltpu.CompilerParams(vmem_limit_bytes=mib << 20)


def f32(*shape):
    return jax.ShapeDtypeStruct(shape, jnp.float32)


def bf16(*shape):
    return jax.ShapeDtypeStruct(shape, jnp.bfloat16)


def body(
    kernels, tile_owner, tile_source, tile_target, tile_seed, tile_count, prev_gradient,
    prev_step, precond,
):
    events, comps, eblocks, nodes = kernels.shape
    parts = lax.axis_size("mesh")
    evs = lax.axis_size("ev")
    group = precond.shape[2]
    subs = group * evs
    blocks = parts * subs
    half = parts // 2
    rows = comps * group
    part_rows = comps * subs
    tiles = tile_source.shape[1]
    dims = dict(field=kernels.shape, half=half, subs=subs, blocks=blocks, tiles=tiles)

    def swap(x, axis, k):
        size = parts if axis == "mesh" else evs
        return lax.ppermute(x, axis, [(i, i ^ k) for i in range(size)])

    owners = jnp.transpose(tile_owner, (0, 2, 1))
    counts = jnp.transpose(tile_count)
    table = bf16(SHAPES * nodes, nodes)
    code_rows = (CODES * events * tiles // LANES, LANES)
    codes_shape = jax.ShapeDtypeStruct(code_rows, jnp.int32)

    packed = pl.pallas_call(
        functools.partial(pack_kernel, comps, group),
        out_shape=f32(3, rows, nodes),
        in_specs=[in_vmem()] * 3,
        out_specs=in_vmem(),
        scratch_shapes=[pltpu.VMEM((group * PITCH, nodes), jnp.float32)],
        compiler_params=limit(2),
        name="pack",
    )(prev_gradient, prev_step, precond)
    hist = [packed]
    for k in range(1, evs):
        hist.append(swap(packed, "ev", k))
    hist = jnp.stack(hist)

    tab = pl.pallas_call(
        functools.partial(table_kernel, nodes),
        out_shape=table,
        out_specs=in_vmem(),
        compiler_params=limit(1),
        cost_estimate=pl.CostEstimate(flops=1 << 28, bytes_accessed=4 << 20, transcendentals=0),
        name="table",
    )()
    sums, codes = pl.pallas_call(
        functools.partial(forward_kernel, dims),
        out_shape=[f32(blocks * comps + ROW, nodes), codes_shape],
        in_specs=[in_smem()] + [in_vmem()] * 6,
        out_specs=[in_vmem()] * 2,
        scratch_shapes=[
            pltpu.VMEM((events * eblocks * PITCH + ROW, nodes), jnp.float32),
            pltpu.SMEM(code_rows, jnp.int32),
            pltpu.SemaphoreType.DMA((1,)),
        ],
        compiler_params=limit(20),
        cost_estimate=pl.CostEstimate(
            flops=2 * events * tiles * ROW * nodes * nodes * 64,
            bytes_accessed=16 << 20,
            transcendentals=0,
        ),
        name="forward",
    )(counts, owners, tile_target, tile_source, tile_seed, kernels, tab)

    keep = sums[: half * part_rows].reshape(half, part_rows, nodes)
    send = sums[half * part_rows : 2 * half * part_rows].reshape(half, part_rows, nodes)
    got = swap(send, "mesh", 1)
    held = [None] + [keep[j] + got[j] for j in range(1, half)]
    arrived = []
    for j in range(1, half):
        arrived.append(swap(held[j], "mesh", 2 * j))
    total = keep[0] + got[0]
    for piece in arrived:
        total = total + piece
    bits = evs.bit_length() - 1
    for bit in range(bits - 1):
        total = total + swap(total, "ev", 1 << bit)
    across = swap(total, "ev", 1 << (bits - 1))

    local = pl.pallas_call(
        functools.partial(sums_kernel, rows, evs),
        out_shape=f32(8, nodes),
        in_specs=[in_vmem()] * 3,
        out_specs=in_vmem(),
        compiler_params=limit(4),
        name="sums",
    )(total, across, hist)
    local = local + swap(local, "mesh", 1)
    spread = [local] + [swap(local, "mesh", 2 * j) for j in range(1, half)]
    inversion_direction, rounded = pl.pallas_call(
        functools.partial(direction_kernel, rows, evs, comps, group),
        out_shape=[f32(*precond.shape), bf16(part_rows, nodes)],
        in_specs=[in_vmem()] * (3 + half),
        out_specs=[in_vmem()] * 2,
        scratch_shapes=[pltpu.VMEM((group * PITCH, nodes), jnp.float32)],
        compiler_params=limit(4),
        name="direction",
    )(total, across, hist, *spread)

    mine = [rounded] + [swap(rounded, "mesh", 2 * j) for j in range(1, half)]
    other = swap(jnp.stack(mine), "mesh", 1)

    event_direction = pl.pallas_call(
        functools.partial(backward_kernel, dims),
        out_shape=f32(*kernels.shape),
        in_specs=[in_smem()] + [in_vmem()] * (half + 3),
        out_specs=in_hbm(),
        scratch_shapes=[
            pltpu.VMEM((blocks * comps + ROW, nodes), jnp.float32),
            pltpu.VMEM((events * eblocks * PITCH + ROW, nodes), jnp.float32),
            pltpu.VMEM(kernels.shape, jnp.float32),
            pltpu.SMEM(code_rows, jnp.int32),
            pltpu.SemaphoreType.DMA((1 + events,)),
        ],
        compiler_params=limit(24),
        name="backward",
    )(counts, codes, tab, *mine, other)
    return inversion_direction, event_direction


def solution(mesh):
    in_specs = (
        P("ev", None, "mesh", None),
        P("ev", "mesh", None),
        P("ev", "mesh"),
        P("ev", "mesh"),
        P("ev", "mesh"),
        P("ev", "mesh"),
        P(None, "mesh", "ev", None),
        P(None, "mesh", "ev", None),
        P(None, "mesh", "ev", None),
    )
    out_specs = (P(None, "mesh", "ev", None), P("ev", None, "mesh", None))

    return jax.shard_map(body, mesh=mesh, in_specs=in_specs, out_specs=out_specs, check_vma=False)
```

```python
import functools

import jax
import jax.numpy as jnp
import numpy as np
from jax import lax
from jax.experimental import pallas as pl
from jax.experimental.pallas import tpu as pltpu
from jax.sharding import PartitionSpec as P


OFFSETS = 7
SPREADS = 3
WEIGHTS = 4
SHAPES = OFFSETS * SPREADS * WEIGHTS
ROW = 16
PITCH = 13
LANES = 128
BAND = 16
CODES = 4


def table_kernel(nodes, tab_ref):
    row = lax.broadcasted_iota(jnp.int32, (8, nodes), 0)
    lane = lax.broadcasted_iota(jnp.int32, (8, nodes), 1)
    signed = jnp.where(lane < nodes // 2, lane, lane - nodes)

    def one(k, carry):
        spread = 0.55 + 0.1 * k.astype(jnp.float32)
        for o in range(OFFSETS):
            distance = (row - signed - (o - OFFSETS // 2)).astype(jnp.float32)
            base = jnp.exp(-distance * distance / (2.0 * spread * spread))
            bells = []
            for i in range(0, nodes, 8):
                bell = base if i == 0 else pltpu.roll(base, i, 1)
                if i < 2 * BAND or i >= nodes - 2 * BAND:
                    near = jnp.abs(row + i - lane) < nodes // 2
                    bell = jnp.where(near, bell, 0.0)
                bells.append(bell)
            for w in range(WEIGHTS):
                weight = np.float32(0.1) + np.float32(0.1) * np.float32(w)
                first = (k + w * SPREADS) * (OFFSETS * nodes) + o * nodes
                for i in range(0, len(bells), 2):
                    pair = jnp.concatenate([weight * bells[i], weight * bells[i + 1]], axis=0)
                    at = pl.ds(pl.multiple_of(first + i * 8, ROW), ROW)
                    tab_ref[at, :] = pair.astype(jnp.bfloat16)
        return carry

    lax.fori_loop(0, SPREADS, one, 0)


def fill_codes(dims, counts, owner_ref, target_ref, source_ref, seed_ref, codes_ref):
    events, comps, eblocks, nodes = dims["field"]
    half, subs, blocks = dims["half"], dims["subs"], dims["blocks"]
    groups = dims["tiles"] // LANES
    lists = events * groups
    me = lax.axis_index("mesh")
    lane = lax.broadcasted_iota(jnp.int32, (1, LANES), 1)
    for v in range(events):
        for g in range(groups):
            at = pl.ds(g * LANES, LANES)
            live = lane + g * LANES < counts[v]
            r = owner_ref[v, :, at] ^ me
            slot = ((r & 1) * half + (r >> 1)) * subs + target_ref[pl.ds(v, 1), at]
            source = source_ref[pl.ds(v, 1), at] + v * eblocks
            seed = seed_ref[pl.ds(v, 1), at]
            turned = 2 * OFFSETS * ((seed * 9363) >> 16) - seed + (OFFSETS - 1)
            codes = (
                jnp.where(live, source, events * eblocks) * PITCH,
                jnp.where(live, slot, blocks) * comps,
                seed * nodes,
                turned * nodes,
            )
            for n, code in enumerate(codes):
                codes_ref[pl.ds(n * lists + v * groups + g, 1), :] = code


def tile_loop(v, count, groups, load, add):
    def group(i, carry):
        results = []
        for u in range(0, LANES, 2):
            x0, g0 = load(v * groups + i, u)
            x1, g1 = load(v * groups + i, u + 1)
            y = jnp.dot(
                jnp.concatenate([x0, x1], axis=0),
                jnp.concatenate([g0, g1], axis=1),
                preferred_element_type=jnp.float32,
            )
            results += [y[:ROW, :LANES], y[ROW:, LANES:]]
        for u in range(LANES):
            add(v * groups + i, u, results[u])
        return carry

    lax.fori_loop(0, (count + LANES - 1) // LANES, group, 0)


def forward_kernel(
    dims, count_ref, owner_ref, target_ref, source_ref, seed_ref, field_ref, tab_ref,
    sum_ref, codes_ref, rows_ref, code_ref, sems,
):
    events, comps, eblocks, nodes = dims["field"]
    groups = dims["tiles"] // LANES
    lists = events * groups
    counts = [count_ref[0, v] for v in range(events)]
    fill_codes(dims, counts, owner_ref, target_ref, source_ref, seed_ref, codes_ref)
    sum_ref[...] = jnp.zeros_like(sum_ref)
    to_smem = pltpu.make_async_copy(codes_ref, code_ref, sems.at[0])
    to_smem.start()
    for v in range(events):
        for c in range(comps):
            rows_ref[pl.ds(v * eblocks * PITCH + c, eblocks, stride=PITCH), :] = field_ref[
                v, c
            ].astype(jnp.float32)
    to_smem.wait()

    def load(i, u):
        shape = pl.multiple_of(code_ref[2 * lists + i, u], nodes)
        x = rows_ref[pl.ds(code_ref[i, u], ROW), :]
        return x.astype(jnp.bfloat16), tab_ref[pl.ds(shape, nodes), :]

    def add(i, u, y):
        at = pl.ds(pl.multiple_of(code_ref[lists + i, u], 4), comps)
        y = y.astype(jnp.bfloat16).astype(jnp.float32)
        sum_ref[at, :] = sum_ref[at, :] + y[:comps]

    for v in range(events):
        tile_loop(v, counts[v], groups, load, add)


def backward_kernel(dims, count_ref, codes_in, tab_ref, *refs):
    events, comps, eblocks, nodes = dims["field"]
    half, subs = dims["half"], dims["subs"]
    groups = dims["tiles"] // LANES
    lists = events * groups
    mine_refs, (other_ref, out_ref, rows_ref, sum_ref, tile_ref, code_ref, sems) = (
        refs[:half], refs[half:],
    )
    to_smem = pltpu.make_async_copy(codes_in, code_ref, sems.at[0])
    to_smem.start()
    sum_ref[...] = jnp.zeros_like(sum_ref)
    part = subs * comps
    for j in range(half):
        rows_ref[pl.ds(j * part, part), :] = mine_refs[j][...].astype(jnp.float32)
        rows_ref[pl.ds((half + j) * part, part), :] = other_ref[j].astype(jnp.float32)
    to_smem.wait()

    def load(i, u):
        shape = pl.multiple_of(code_ref[3 * lists + i, u], nodes)
        x = rows_ref[pl.ds(pl.multiple_of(code_ref[lists + i, u], 4), ROW), :]
        return x.astype(jnp.bfloat16), tab_ref[pl.ds(shape, nodes), :]

    def add(i, u, y):
        at = pl.ds(code_ref[i, u], comps)
        sum_ref[at, :] = sum_ref[at, :] + y[:comps]

    sends = []
    for v in range(events):
        tile_loop(v, count_ref[0, v], groups, load, add)
        for c in range(comps):
            tile_ref[v, c] = sum_ref[pl.ds(v * eblocks * PITCH + c, eblocks, stride=PITCH), :]
        send = pltpu.make_async_copy(tile_ref.at[v], out_ref.at[v], sems.at[1 + v])
        send.start()
        sends.append(send)
    for send in sends:
        send.wait()


def pack_kernel(comps, group, *refs):
    ins, (out_ref, wide_ref) = refs[:-2], refs[-2:]
    for n, ref in enumerate(ins):
        for c in range(comps):
            wide_ref[pl.ds(c, group, stride=PITCH), :] = ref[c, 0]
        for s in range(group):
            out_ref[n, pl.ds(s * comps, comps), :] = wide_ref[pl.ds(s * PITCH, comps), :]


def fold_kernel(a_ref, b_ref, out_ref):
    out_ref[...] = a_ref[...] + b_ref[...]


def terms(a_ref, b_ref, hist_ref, k, rows):
    group = lax.axis_index("ev") ^ k
    at = pl.ds(pl.multiple_of(group * rows, 8), rows)
    gradient = a_ref[at, :] + b_ref[at, :]
    prev_gradient, prev_step, precond = hist_ref[k, 0], hist_ref[k, 1], hist_ref[k, 2]
    return at, gradient, gradient - prev_gradient, prev_step, precond


def sums_kernel(rows, evs, a_ref, b_ref, hist_ref, out_ref):
    total = [jnp.zeros((8, LANES), jnp.float32) for _ in range(4)]
    for k in range(evs):
        _, gradient, change, prev_step, precond = terms(a_ref, b_ref, hist_ref, k, rows)
        weighted = precond * change
        parts = (prev_step * change, prev_step * gradient, weighted * gradient, weighted * change)
        for n, part in enumerate(parts):
            total[n] = total[n] + jnp.sum(part.reshape(rows // 8, 8, LANES), axis=0)
    for n in range(4):
        out_ref[pl.ds(n, 1), :] = jnp.sum(total[n], axis=0, keepdims=True)
    out_ref[pl.ds(4, 4), :] = jnp.zeros((4, LANES), jnp.float32)


def direction_kernel(rows, evs, a_ref, b_ref, hist_ref, *refs):
    sum_refs, (inv_ref, round_ref) = refs[:-2], refs[-2:]
    level = [ref[...] for ref in sum_refs]
    while len(level) > 1:
        level = [level[i] + level[i + 1] for i in range(0, len(level), 2)]
    sums = jnp.sum(level[0], axis=1, keepdims=True)
    curvature, slope, cross_term, self_term = (sums[n : n + 1] for n in range(4))
    alpha = slope / curvature
    beta = (cross_term - alpha * self_term) / curvature
    bend = alpha - beta
    for k in range(evs):
        at, gradient, change, prev_step, precond = terms(a_ref, b_ref, hist_ref, k, rows)
        scaled = precond * (gradient - alpha * change)
        direction = -(scaled + bend * prev_step)
        round_ref[at, :] = direction.astype(jnp.bfloat16)
        if k == 0:
            inv_ref[...] = direction


def unpack_kernel(comps, group, in_ref, out_ref, wide_ref):
    for s in range(group):
        wide_ref[pl.ds(s * PITCH, comps), :] = in_ref[pl.ds(s * comps, comps), :]
    for c in range(comps):
        out_ref[c, 0] = wide_ref[pl.ds(c, group, stride=PITCH), :]


def in_smem():
    return pl.BlockSpec(memory_space=pltpu.SMEM)


def in_vmem():
    return pl.BlockSpec(memory_space=pltpu.VMEM)


def in_hbm():
    return pl.BlockSpec(memory_space=pltpu.HBM)


def limit(mib):
    return pltpu.CompilerParams(vmem_limit_bytes=mib << 20)


def f32(*shape):
    return jax.ShapeDtypeStruct(shape, jnp.float32)


def bf16(*shape):
    return jax.ShapeDtypeStruct(shape, jnp.bfloat16)


def body(
    kernels, tile_owner, tile_source, tile_target, tile_seed, tile_count, prev_gradient,
    prev_step, precond,
):
    events, comps, eblocks, nodes = kernels.shape
    parts = lax.axis_size("mesh")
    evs = lax.axis_size("ev")
    group = precond.shape[2]
    subs = group * evs
    blocks = parts * subs
    half = parts // 2
    rows = comps * group
    part_rows = comps * subs
    tiles = tile_source.shape[1]
    dims = dict(field=kernels.shape, half=half, subs=subs, blocks=blocks, tiles=tiles)

    def swap(x, axis, k):
        size = parts if axis == "mesh" else evs
        return lax.ppermute(x, axis, [(i, i ^ k) for i in range(size)])

    owners = jnp.transpose(tile_owner, (0, 2, 1))
    counts = jnp.transpose(tile_count)
    table = bf16(SHAPES * nodes, nodes)
    code_rows = (CODES * events * tiles // LANES, LANES)
    codes_shape = jax.ShapeDtypeStruct(code_rows, jnp.int32)

    packed = pl.pallas_call(
        functools.partial(pack_kernel, comps, group),
        out_shape=f32(3, rows, nodes),
        in_specs=[in_vmem()] * 3,
        out_specs=in_vmem(),
        scratch_shapes=[pltpu.VMEM((group * PITCH, nodes), jnp.float32)],
        compiler_params=limit(2),
        name="pack",
    )(prev_gradient, prev_step, precond)
    hist = packed[None]
    for bit in range(evs.bit_length() - 1):
        hist = jnp.concatenate([hist, swap(hist, "ev", 1 << bit)], axis=0)

    tab = pl.pallas_call(
        functools.partial(table_kernel, nodes),
        out_shape=table,
        out_specs=in_vmem(),
        compiler_params=limit(1),
        cost_estimate=pl.CostEstimate(flops=1 << 28, bytes_accessed=4 << 20, transcendentals=0),
        name="table",
    )()
    sums, codes = pl.pallas_call(
        functools.partial(forward_kernel, dims),
        out_shape=[f32(blocks * comps + ROW, nodes), codes_shape],
        in_specs=[in_smem()] + [in_vmem()] * 6,
        out_specs=[in_vmem()] * 2,
        scratch_shapes=[
            pltpu.VMEM((events * eblocks * PITCH + ROW, nodes), jnp.float32),
            pltpu.SMEM(code_rows, jnp.int32),
            pltpu.SemaphoreType.DMA((1,)),
        ],
        compiler_params=limit(20),
        cost_estimate=pl.CostEstimate(
            flops=2 * events * tiles * ROW * nodes * nodes * 64,
            bytes_accessed=16 << 20,
            transcendentals=0,
        ),
        name="forward",
    )(counts, owners, tile_target, tile_source, tile_seed, kernels, tab)

    keep = sums[: half * part_rows].reshape(half, part_rows, nodes)
    send = sums[half * part_rows : 2 * half * part_rows].reshape(half, part_rows, nodes)
    got = swap(send, "mesh", 1)
    held = [None] + [keep[j] + got[j] for j in range(1, half)]
    arrived = []
    for j in range(1, half):
        arrived.append(swap(held[j], "mesh", 2 * j))
    total = pl.pallas_call(
        fold_kernel,
        out_shape=f32(part_rows, nodes),
        in_specs=[in_vmem()] * 2,
        out_specs=in_vmem(),
        compiler_params=limit(2),
        name="fold",
    )(keep[0], got[0])
    for piece in arrived:
        total = total + piece
    bits = evs.bit_length() - 1
    for bit in range(bits - 1):
        total = total + swap(total, "ev", 1 << bit)
    across = swap(total, "ev", 1 << (bits - 1))

    local = pl.pallas_call(
        functools.partial(sums_kernel, rows, evs),
        out_shape=f32(8, nodes),
        in_specs=[in_vmem()] * 3,
        out_specs=in_vmem(),
        compiler_params=limit(4),
        name="sums",
    )(total, across, hist)
    local = local + swap(local, "mesh", 1)
    spread = [local] + [swap(local, "mesh", 2 * j) for j in range(1, half)]
    inverse, rounded = pl.pallas_call(
        functools.partial(direction_kernel, rows, evs),
        out_shape=[f32(rows, nodes), bf16(part_rows, nodes)],
        in_specs=[in_vmem()] * (3 + half),
        out_specs=[in_vmem()] * 2,
        compiler_params=limit(4),
        name="direction",
    )(total, across, hist, *spread)
    inversion_direction = pl.pallas_call(
        functools.partial(unpack_kernel, comps, group),
        out_shape=f32(*precond.shape),
        in_specs=[in_vmem()],
        out_specs=in_vmem(),
        scratch_shapes=[pltpu.VMEM((group * PITCH, nodes), jnp.float32)],
        compiler_params=limit(2),
        name="unpack",
    )(inverse)

    mine = [rounded]
    for j in range(1, half):
        mine.append(swap(rounded, "mesh", 2 * j))
    other = swap(jnp.stack(mine), "mesh", 1)

    event_direction = pl.pallas_call(
        functools.partial(backward_kernel, dims),
        out_shape=f32(*kernels.shape),
        in_specs=[in_smem()] + [in_vmem()] * (half + 3),
        out_specs=in_hbm(),
        scratch_shapes=[
            pltpu.VMEM((blocks * comps + ROW, nodes), jnp.float32),
            pltpu.VMEM((events * eblocks * PITCH + ROW, nodes), jnp.float32),
            pltpu.VMEM(kernels.shape, jnp.float32),
            pltpu.SMEM(code_rows, jnp.int32),
            pltpu.SemaphoreType.DMA((1 + events,)),
        ],
        compiler_params=limit(24),
        name="backward",
    )(counts, codes, tab, *mine, other)
    return inversion_direction, event_direction


def solution(mesh):
    in_specs = (
        P("ev", None, "mesh", None),
        P("ev", "mesh", None),
        P("ev", "mesh"),
        P("ev", "mesh"),
        P("ev", "mesh"),
        P("ev", "mesh"),
        P(None, "mesh", "ev", None),
        P(None, "mesh", "ev", None),
        P(None, "mesh", "ev", None),
    )
    out_specs = (P(None, "mesh", "ev", None), P("ev", None, "mesh", None))

    return jax.shard_map(body, mesh=mesh, in_specs=in_specs, out_specs=out_specs, check_vma=False)
```

```python
import functools

import jax
import jax.numpy as jnp
import numpy as np
from jax import lax
from jax.experimental import pallas as pl
from jax.experimental.pallas import tpu as pltpu
from jax.sharding import PartitionSpec as P


OFFSETS = 7
SPREADS = 3
WEIGHTS = 4
SHAPES = OFFSETS * SPREADS * WEIGHTS
ROW = 16
PITCH = 13
LANES = 128
BAND = 16
CODES = 4


def table_kernel(nodes, tab_ref):
    row = lax.broadcasted_iota(jnp.int32, (8, nodes), 0)
    lane = lax.broadcasted_iota(jnp.int32, (8, nodes), 1)
    signed = jnp.where(lane < nodes // 2, lane, lane - nodes)

    def one(k, carry):
        spread = 0.55 + 0.1 * k.astype(jnp.float32)
        for o in range(OFFSETS):
            distance = (row - signed - (o - OFFSETS // 2)).astype(jnp.float32)
            base = jnp.exp(-distance * distance / (2.0 * spread * spread))
            bells = []
            for i in range(0, nodes, 8):
                bell = base if i == 0 else pltpu.roll(base, i, 1)
                if i < 2 * BAND or i >= nodes - 2 * BAND:
                    near = jnp.abs(row + i - lane) < nodes // 2
                    bell = jnp.where(near, bell, 0.0)
                bells.append(bell)
            for w in range(WEIGHTS):
                weight = np.float32(0.1) + np.float32(0.1) * np.float32(w)
                first = (k + w * SPREADS) * (OFFSETS * nodes) + o * nodes
                for i in range(0, len(bells), 2):
                    pair = jnp.concatenate([weight * bells[i], weight * bells[i + 1]], axis=0)
                    at = pl.ds(pl.multiple_of(first + i * 8, ROW), ROW)
                    tab_ref[at, :] = pair.astype(jnp.bfloat16)
        return carry

    lax.fori_loop(0, SPREADS, one, 0)


def fill_codes(dims, counts, owner_ref, target_ref, source_ref, seed_ref, codes_ref):
    events, comps, eblocks, nodes = dims["field"]
    half, subs, blocks = dims["half"], dims["subs"], dims["blocks"]
    groups = dims["tiles"] // LANES
    lists = events * groups
    me = lax.axis_index("mesh")
    lane = lax.broadcasted_iota(jnp.int32, (1, LANES), 1)
    for v in range(events):
        for g in range(groups):
            at = pl.ds(g * LANES, LANES)
            live = lane + g * LANES < counts[v]
            r = owner_ref[v, :, at] ^ me
            slot = ((r & 1) * half + (r >> 1)) * subs + target_ref[pl.ds(v, 1), at]
            source = source_ref[pl.ds(v, 1), at] + v * eblocks
            seed = seed_ref[pl.ds(v, 1), at]
            turned = 2 * OFFSETS * ((seed * 9363) >> 16) - seed + (OFFSETS - 1)
            codes = (
                jnp.where(live, source, events * eblocks) * PITCH,
                jnp.where(live, slot, blocks) * comps,
                seed * nodes,
                turned * nodes,
            )
            for n, code in enumerate(codes):
                codes_ref[pl.ds(n * lists + v * groups + g, 1), :] = code


def tile_loop(v, count, groups, load, add):
    def group(i, carry):
        results = []
        for u in range(0, LANES, 2):
            x0, g0 = load(v * groups + i, u)
            x1, g1 = load(v * groups + i, u + 1)
            y = jnp.dot(
                jnp.concatenate([x0, x1], axis=0),
                jnp.concatenate([g0, g1], axis=1),
                preferred_element_type=jnp.float32,
            )
            results += [y[:ROW, :LANES], y[ROW:, LANES:]]
        for u in range(LANES):
            add(v * groups + i, u, results[u])
        return carry

    lax.fori_loop(0, (count + LANES - 1) // LANES, group, 0)


def forward_kernel(
    dims, count_ref, owner_ref, target_ref, source_ref, seed_ref, field_ref, tab_ref,
    sum_ref, codes_ref, rows_ref, code_ref, sems,
):
    events, comps, eblocks, nodes = dims["field"]
    groups = dims["tiles"] // LANES
    lists = events * groups
    counts = [count_ref[0, v] for v in range(events)]
    fill_codes(dims, counts, owner_ref, target_ref, source_ref, seed_ref, codes_ref)
    sum_ref[...] = jnp.zeros_like(sum_ref)
    to_smem = pltpu.make_async_copy(codes_ref, code_ref, sems.at[0])
    to_smem.start()
    for v in range(events):
        for c in range(comps):
            rows_ref[pl.ds(v * eblocks * PITCH + c, eblocks, stride=PITCH), :] = field_ref[
                v, c
            ].astype(jnp.float32)
    to_smem.wait()

    def load(i, u):
        shape = pl.multiple_of(code_ref[2 * lists + i, u], nodes)
        x = rows_ref[pl.ds(code_ref[i, u], ROW), :]
        return x.astype(jnp.bfloat16), tab_ref[pl.ds(shape, nodes), :]

    def add(i, u, y):
        at = pl.ds(pl.multiple_of(code_ref[lists + i, u], 4), comps)
        y = y.astype(jnp.bfloat16).astype(jnp.float32)
        sum_ref[at, :] = sum_ref[at, :] + y[:comps]

    for v in range(events):
        tile_loop(v, counts[v], groups, load, add)


def backward_kernel(dims, count_ref, codes_in, tab_ref, *refs):
    events, comps, eblocks, nodes = dims["field"]
    half, subs = dims["half"], dims["subs"]
    groups = dims["tiles"] // LANES
    lists = events * groups
    mine_refs, (other_ref, out_ref, rows_ref, sum_ref, tile_ref, code_ref, sems) = (
        refs[:half], refs[half:],
    )
    to_smem = pltpu.make_async_copy(codes_in, code_ref, sems.at[0])
    to_smem.start()
    sum_ref[...] = jnp.zeros_like(sum_ref)
    part = subs * comps
    for j in range(half):
        rows_ref[pl.ds(j * part, part), :] = mine_refs[j][...].astype(jnp.float32)
        rows_ref[pl.ds((half + j) * part, part), :] = other_ref[j].astype(jnp.float32)
    to_smem.wait()

    def load(i, u):
        shape = pl.multiple_of(code_ref[3 * lists + i, u], nodes)
        x = rows_ref[pl.ds(pl.multiple_of(code_ref[lists + i, u], 4), ROW), :]
        return x.astype(jnp.bfloat16), tab_ref[pl.ds(shape, nodes), :]

    def add(i, u, y):
        at = pl.ds(code_ref[i, u], comps)
        sum_ref[at, :] = sum_ref[at, :] + y[:comps]

    sends = []
    for v in range(events):
        tile_loop(v, count_ref[0, v], groups, load, add)
        for c in range(comps):
            tile_ref[v, c] = sum_ref[pl.ds(v * eblocks * PITCH + c, eblocks, stride=PITCH), :]
        send = pltpu.make_async_copy(tile_ref.at[v], out_ref.at[v], sems.at[1 + v])
        send.start()
        sends.append(send)
    for send in sends:
        send.wait()


def pack_kernel(comps, group, *refs):
    ins, (out_ref, wide_ref) = refs[:-2], refs[-2:]
    for n, ref in enumerate(ins):
        for c in range(comps):
            wide_ref[pl.ds(c, group, stride=PITCH), :] = ref[c, 0]
        for s in range(group):
            out_ref[n, pl.ds(s * comps, comps), :] = wide_ref[pl.ds(s * PITCH, comps), :]


def fold_kernel(a_ref, b_ref, out_ref):
    out_ref[...] = a_ref[...] + b_ref[...]


def merge_kernel(*refs):
    ins, (stay_ref, go_ref) = refs[:-2], refs[-2:]
    rows = stay_ref.shape[0]
    odd = lax.axis_index("ev") & 1
    for out_ref, part in ((stay_ref, odd), (go_ref, 1 - odd)):
        at = pl.ds(pl.multiple_of(part * rows, 8), rows)
        total = ins[0][at, :]
        for ref in ins[1:]:
            total = total + ref[at, :]
        out_ref[...] = total


def terms(gradient, hist_ref, k):
    prev_gradient, prev_step, precond = hist_ref[k, 0], hist_ref[k, 1], hist_ref[k, 2]
    return gradient - prev_gradient, prev_step, precond


def sums_kernel(rows, evs, a_ref, b_ref, hist_ref, grad_ref, out_ref):
    ev = lax.axis_index("ev")
    grad_ref[...] = a_ref[...] + b_ref[...]
    total = [jnp.zeros((8, LANES), jnp.float32) for _ in range(4)]
    for i in range(evs // 2):
        k = ((ev & 1) * (evs // 2) + i) ^ ev
        gradient = grad_ref[pl.ds(i * rows, rows), :]
        change, prev_step, precond = terms(gradient, hist_ref, k)
        weighted = precond * change
        parts = (prev_step * change, prev_step * gradient, weighted * gradient, weighted * change)
        for n, part in enumerate(parts):
            total[n] = total[n] + jnp.sum(part.reshape(rows // 8, 8, LANES), axis=0)
    for n in range(4):
        out_ref[pl.ds(n, 1), :] = jnp.sum(total[n], axis=0, keepdims=True)
    out_ref[pl.ds(4, 4), :] = jnp.zeros((4, LANES), jnp.float32)


def direction_kernel(rows, evs, mine_ref, other_ref, hist_ref, *refs):
    sum_refs, (inv_ref, round_ref, grad_ref) = refs[:-3], refs[-3:]
    ev = lax.axis_index("ev")
    level = [ref[...] for ref in sum_refs]
    while len(level) > 1:
        level = [level[i] + level[i + 1] for i in range(0, len(level), 2)]
    sums = jnp.sum(level[0], axis=1, keepdims=True)
    curvature, slope, cross_term, self_term = (sums[n : n + 1] for n in range(4))
    alpha = slope / curvature
    beta = (cross_term - alpha * self_term) / curvature
    bend = alpha - beta
    half_rows = mine_ref.shape[0]
    for ref, part in ((mine_ref, ev & 1), (other_ref, 1 - (ev & 1))):
        grad_ref[pl.ds(pl.multiple_of(part * half_rows, 8), half_rows), :] = ref[...]
    for k in range(evs):
        at = pl.ds(pl.multiple_of((ev ^ k) * rows, ROW), rows)
        gradient = grad_ref[at, :]
        change, prev_step, precond = terms(gradient, hist_ref, k)
        scaled = precond * (gradient - alpha * change)
        direction = -(scaled + bend * prev_step)
        round_ref[at, :] = direction.astype(jnp.bfloat16)
        if k == 0:
            inv_ref[...] = direction


def unpack_kernel(comps, group, in_ref, out_ref, wide_ref):
    for s in range(group):
        wide_ref[pl.ds(s * PITCH, comps), :] = in_ref[pl.ds(s * comps, comps), :]
    for c in range(comps):
        out_ref[c, 0] = wide_ref[pl.ds(c, group, stride=PITCH), :]


def in_smem():
    return pl.BlockSpec(memory_space=pltpu.SMEM)


def in_vmem():
    return pl.BlockSpec(memory_space=pltpu.VMEM)


def in_hbm():
    return pl.BlockSpec(memory_space=pltpu.HBM)


def limit(mib):
    return pltpu.CompilerParams(vmem_limit_bytes=mib << 20)


def f32(*shape):
    return jax.ShapeDtypeStruct(shape, jnp.float32)


def bf16(*shape):
    return jax.ShapeDtypeStruct(shape, jnp.bfloat16)


def body(
    kernels, tile_owner, tile_source, tile_target, tile_seed, tile_count, prev_gradient,
    prev_step, precond,
):
    events, comps, eblocks, nodes = kernels.shape
    parts = lax.axis_size("mesh")
    evs = lax.axis_size("ev")
    group = precond.shape[2]
    subs = group * evs
    blocks = parts * subs
    half = parts // 2
    rows = comps * group
    part_rows = comps * subs
    tiles = tile_source.shape[1]
    dims = dict(field=kernels.shape, half=half, subs=subs, blocks=blocks, tiles=tiles)

    def swap(x, axis, k):
        size = parts if axis == "mesh" else evs
        return lax.ppermute(x, axis, [(i, i ^ k) for i in range(size)])

    owners = jnp.transpose(tile_owner, (0, 2, 1))
    counts = jnp.transpose(tile_count)
    table = bf16(SHAPES * nodes, nodes)
    code_rows = (CODES * events * tiles // LANES, LANES)
    codes_shape = jax.ShapeDtypeStruct(code_rows, jnp.int32)

    packed = pl.pallas_call(
        functools.partial(pack_kernel, comps, group),
        out_shape=f32(3, rows, nodes),
        in_specs=[in_vmem()] * 3,
        out_specs=in_vmem(),
        scratch_shapes=[pltpu.VMEM((group * PITCH, nodes), jnp.float32)],
        compiler_params=limit(2),
        name="pack",
    )(prev_gradient, prev_step, precond)
    hist = packed[None]
    for bit in range(evs.bit_length() - 1):
        hist = jnp.concatenate([hist, swap(hist, "ev", 1 << bit)], axis=0)

    tab = pl.pallas_call(
        functools.partial(table_kernel, nodes),
        out_shape=table,
        out_specs=in_vmem(),
        compiler_params=limit(1),
        cost_estimate=pl.CostEstimate(flops=1 << 28, bytes_accessed=4 << 20, transcendentals=0),
        name="table",
    )()
    sums, codes = pl.pallas_call(
        functools.partial(forward_kernel, dims),
        out_shape=[f32(blocks * comps + ROW, nodes), codes_shape],
        in_specs=[in_smem()] + [in_vmem()] * 6,
        out_specs=[in_vmem()] * 2,
        scratch_shapes=[
            pltpu.VMEM((events * eblocks * PITCH + ROW, nodes), jnp.float32),
            pltpu.SMEM(code_rows, jnp.int32),
            pltpu.SemaphoreType.DMA((1,)),
        ],
        compiler_params=limit(20),
        cost_estimate=pl.CostEstimate(
            flops=2 * events * tiles * ROW * nodes * nodes * 64,
            bytes_accessed=16 << 20,
            transcendentals=0,
        ),
        name="forward",
    )(counts, owners, tile_target, tile_source, tile_seed, kernels, tab)

    keep = sums[: half * part_rows].reshape(half, part_rows, nodes)
    send = sums[half * part_rows : 2 * half * part_rows].reshape(half, part_rows, nodes)
    got = swap(send, "mesh", 1)
    held = [None] + [keep[j] + got[j] for j in range(1, half)]
    arrived = []
    for j in range(1, half):
        arrived.append(swap(held[j], "mesh", 2 * j))
    total = pl.pallas_call(
        fold_kernel,
        out_shape=f32(part_rows, nodes),
        in_specs=[in_vmem()] * 2,
        out_specs=in_vmem(),
        compiler_params=limit(2),
        name="fold",
    )(keep[0], got[0])
    half_rows = part_rows // 2
    stay, go = pl.pallas_call(
        merge_kernel,
        out_shape=[f32(half_rows, nodes)] * 2,
        in_specs=[in_vmem()] * half,
        out_specs=[in_vmem()] * 2,
        compiler_params=limit(4),
        name="merge",
    )(total, *arrived)
    total, across = stay, swap(go, "ev", 1)
    for bit in range(1, evs.bit_length() - 1):
        total = total + across
        across = swap(total, "ev", 1 << bit)

    gradient, local = pl.pallas_call(
        functools.partial(sums_kernel, rows, evs),
        out_shape=[f32(half_rows, nodes), f32(8, nodes)],
        in_specs=[in_vmem()] * 3,
        out_specs=[in_vmem()] * 2,
        compiler_params=limit(4),
        name="sums",
    )(total, across, hist)
    local = local + swap(local, "ev", 1)
    gradient_other = swap(gradient, "ev", 1)
    local = local + swap(local, "mesh", 1)
    spread = [local] + [swap(local, "mesh", 2 * j) for j in range(1, half)]
    inverse, rounded = pl.pallas_call(
        functools.partial(direction_kernel, rows, evs),
        out_shape=[f32(rows, nodes), bf16(part_rows, nodes)],
        in_specs=[in_vmem()] * (3 + half),
        out_specs=[in_vmem()] * 2,
        scratch_shapes=[pltpu.VMEM((part_rows, nodes), jnp.float32)],
        compiler_params=limit(4),
        name="direction",
    )(gradient, gradient_other, hist, *spread)
    inversion_direction = pl.pallas_call(
        functools.partial(unpack_kernel, comps, group),
        out_shape=f32(*precond.shape),
        in_specs=[in_vmem()],
        out_specs=in_vmem(),
        scratch_shapes=[pltpu.VMEM((group * PITCH, nodes), jnp.float32)],
        compiler_params=limit(2),
        name="unpack",
    )(inverse)

    mine = [rounded]
    for j in range(1, half):
        mine.append(swap(rounded, "mesh", 2 * j))
    other = swap(jnp.stack(mine), "mesh", 1)

    event_direction = pl.pallas_call(
        functools.partial(backward_kernel, dims),
        out_shape=f32(*kernels.shape),
        in_specs=[in_smem()] + [in_vmem()] * (half + 3),
        out_specs=in_hbm(),
        scratch_shapes=[
            pltpu.VMEM((blocks * comps + ROW, nodes), jnp.float32),
            pltpu.VMEM((events * eblocks * PITCH + ROW, nodes), jnp.float32),
            pltpu.VMEM(kernels.shape, jnp.float32),
            pltpu.SMEM(code_rows, jnp.int32),
            pltpu.SemaphoreType.DMA((1 + events,)),
        ],
        compiler_params=limit(24),
        name="backward",
    )(counts, codes, tab, *mine, other)
    return inversion_direction, event_direction


def solution(mesh):
    in_specs = (
        P("ev", None, "mesh", None),
        P("ev", "mesh", None),
        P("ev", "mesh"),
        P("ev", "mesh"),
        P("ev", "mesh"),
        P("ev", "mesh"),
        P(None, "mesh", "ev", None),
        P(None, "mesh", "ev", None),
        P(None, "mesh", "ev", None),
    )
    out_specs = (P(None, "mesh", "ev", None), P("ev", None, "mesh", None))

    return jax.shard_map(body, mesh=mesh, in_specs=in_specs, out_specs=out_specs, check_vma=False)
```

```python
import functools
import math

import jax
import jax.numpy as jnp
import numpy as np
from jax import lax
from jax.experimental import pallas as pl
from jax.experimental.pallas import tpu as pltpu
from jax.sharding import PartitionSpec as P


OFFSETS = 7
SPREADS = 3
WEIGHTS = 4
SHAPES = OFFSETS * SPREADS * WEIGHTS
ROW = 16
PITCH = 13
LANES = 128
BAND = 16
CODES = 4
BODY = 2


def table_kernel(nodes, tab_ref):
    row = lax.broadcasted_iota(jnp.int32, (8, nodes), 0)
    lane = lax.broadcasted_iota(jnp.int32, (8, nodes), 1)
    signed = jnp.where(lane < nodes // 2, lane, lane - nodes)

    def one(k, carry):
        spread = 0.55 + 0.1 * k.astype(jnp.float32)
        for o in range(OFFSETS):
            distance = (row - signed - (o - OFFSETS // 2)).astype(jnp.float32)
            base = jnp.exp(-distance * distance / (2.0 * spread * spread))
            bells = []
            for i in range(0, nodes, 8):
                bell = base if i == 0 else pltpu.roll(base, i, 1)
                if i < 2 * BAND or i >= nodes - 2 * BAND:
                    near = jnp.abs(row + i - lane) < nodes // 2
                    bell = jnp.where(near, bell, 0.0)
                bells.append(bell)
            for w in range(WEIGHTS):
                weight = np.float32(0.1) + np.float32(0.1) * np.float32(w)
                first = (k + w * SPREADS) * (OFFSETS * nodes) + o * nodes
                for i in range(0, len(bells), 2):
                    pair = jnp.concatenate([weight * bells[i], weight * bells[i + 1]], axis=0)
                    at = pl.ds(pl.multiple_of(first + i * 8, ROW), ROW)
                    tab_ref[at, :] = pair.astype(jnp.bfloat16)
        return carry

    lax.fori_loop(0, SPREADS, one, 0)


def fill_codes(dims, counts, owner_ref, target_ref, source_ref, seed_ref, codes_ref):
    events, comps, eblocks, nodes = dims["field"]
    half, subs, blocks = dims["half"], dims["subs"], dims["blocks"]
    groups = dims["tiles"] // LANES
    lists = events * groups
    me = lax.axis_index("mesh")
    lane = lax.broadcasted_iota(jnp.int32, (1, LANES), 1)
    for v in range(events):
        for g in range(groups):
            at = pl.ds(g * LANES, LANES)
            live = lane + g * LANES < counts[v]
            r = owner_ref[v, :, at] ^ me
            slot = ((r & 1) * half + (r >> 1)) * subs + target_ref[pl.ds(v, 1), at]
            source = source_ref[pl.ds(v, 1), at] + v * eblocks
            seed = seed_ref[pl.ds(v, 1), at]
            turned = 2 * OFFSETS * ((seed * 9363) >> 16) - seed + (OFFSETS - 1)
            codes = (
                jnp.where(live, source, events * eblocks) * PITCH,
                jnp.where(live, slot, blocks) * comps,
                seed * nodes,
                turned * nodes,
            )
            for n, code in enumerate(codes):
                codes_ref[pl.ds(n * lists + v * groups + g, 1), :] = code


def tile_loop(v, count, groups, load, add):
    body = math.gcd(BODY, groups)

    def group(i, carry):
        first = v * groups + i * body
        places = [(first + p, u) for p in range(body) for u in range(LANES)]
        results = []
        for n in range(0, len(places), 2):
            x0, g0 = load(*places[n])
            x1, g1 = load(*places[n + 1])
            y = jnp.dot(
                jnp.concatenate([x0, x1], axis=0),
                jnp.concatenate([g0, g1], axis=1),
                preferred_element_type=jnp.float32,
            )
            results += [y[:ROW, :LANES], y[ROW:, LANES:]]
        for place, y in zip(places, results):
            add(*place, y)
        return carry

    size = body * LANES
    lax.fori_loop(0, (count + size - 1) // size, group, 0)


def forward_kernel(
    dims, count_ref, owner_ref, target_ref, source_ref, seed_ref, field_ref, tab_ref,
    sum_ref, codes_ref, rows_ref, code_ref, sems,
):
    events, comps, eblocks, nodes = dims["field"]
    groups = dims["tiles"] // LANES
    lists = events * groups
    counts = [count_ref[0, v] for v in range(events)]
    fill_codes(dims, counts, owner_ref, target_ref, source_ref, seed_ref, codes_ref)
    sum_ref[...] = jnp.zeros_like(sum_ref)
    to_smem = pltpu.make_async_copy(codes_ref, code_ref, sems.at[0])
    to_smem.start()
    for v in range(events):
        for c in range(comps):
            rows_ref[pl.ds(v * eblocks * PITCH + c, eblocks, stride=PITCH), :] = field_ref[
                v, c
            ].astype(jnp.float32)
    to_smem.wait()

    def load(i, u):
        shape = pl.multiple_of(code_ref[2 * lists + i, u], nodes)
        x = rows_ref[pl.ds(code_ref[i, u], ROW), :]
        return x.astype(jnp.bfloat16), tab_ref[pl.ds(shape, nodes), :]

    def add(i, u, y):
        at = pl.ds(pl.multiple_of(code_ref[lists + i, u], 4), comps)
        y = y.astype(jnp.bfloat16).astype(jnp.float32)
        sum_ref[at, :] = sum_ref[at, :] + y[:comps]

    for v in range(events):
        tile_loop(v, counts[v], groups, load, add)


def backward_kernel(dims, count_ref, codes_in, tab_ref, *refs):
    events, comps, eblocks, nodes = dims["field"]
    half, subs = dims["half"], dims["subs"]
    groups = dims["tiles"] // LANES
    lists = events * groups
    mine_refs, (other_ref, out_ref, rows_ref, sum_ref, tile_ref, code_ref, sems) = (
        refs[:half], refs[half:],
    )
    to_smem = pltpu.make_async_copy(codes_in, code_ref, sems.at[0])
    to_smem.start()
    sum_ref[...] = jnp.zeros_like(sum_ref)
    part = subs * comps
    for j in range(half):
        rows_ref[pl.ds(j * part, part), :] = mine_refs[j][...].astype(jnp.float32)
        rows_ref[pl.ds((half + j) * part, part), :] = other_ref[j].astype(jnp.float32)
    to_smem.wait()

    def load(i, u):
        shape = pl.multiple_of(code_ref[3 * lists + i, u], nodes)
        x = rows_ref[pl.ds(pl.multiple_of(code_ref[lists + i, u], 4), ROW), :]
        return x.astype(jnp.bfloat16), tab_ref[pl.ds(shape, nodes), :]

    def add(i, u, y):
        at = pl.ds(code_ref[i, u], comps)
        sum_ref[at, :] = sum_ref[at, :] + y[:comps]

    sends = []
    for v in range(events):
        tile_loop(v, count_ref[0, v], groups, load, add)
        for c in range(comps):
            tile_ref[v, c] = sum_ref[pl.ds(v * eblocks * PITCH + c, eblocks, stride=PITCH), :]
        send = pltpu.make_async_copy(tile_ref.at[v], out_ref.at[v], sems.at[1 + v])
        send.start()
        sends.append(send)
    for send in sends:
        send.wait()


def pack_kernel(comps, group, *refs):
    ins, (out_ref, wide_ref) = refs[:-2], refs[-2:]
    for n, ref in enumerate(ins):
        for c in range(comps):
            wide_ref[pl.ds(c, group, stride=PITCH), :] = ref[c, 0]
        for s in range(group):
            out_ref[n, pl.ds(s * comps, comps), :] = wide_ref[pl.ds(s * PITCH, comps), :]


def fold_kernel(a_ref, b_ref, out_ref):
    out_ref[...] = a_ref[...] + b_ref[...]


def merge_kernel(*refs):
    ins, (stay_ref, go_ref) = refs[:-2], refs[-2:]
    rows = stay_ref.shape[0]
    odd = lax.axis_index("ev") & 1
    for out_ref, part in ((stay_ref, odd), (go_ref, 1 - odd)):
        at = pl.ds(pl.multiple_of(part * rows, 8), rows)
        total = ins[0][at, :]
        for ref in ins[1:]:
            total = total + ref[at, :]
        out_ref[...] = total


def terms(gradient, hist_ref, k):
    prev_gradient, prev_step, precond = hist_ref[k, 0], hist_ref[k, 1], hist_ref[k, 2]
    return gradient - prev_gradient, prev_step, precond


def sums_kernel(rows, evs, a_ref, b_ref, hist_ref, grad_ref, out_ref):
    ev = lax.axis_index("ev")
    grad_ref[...] = a_ref[...] + b_ref[...]
    total = [jnp.zeros((8, LANES), jnp.float32) for _ in range(4)]
    for i in range(evs // 2):
        k = ((ev & 1) * (evs // 2) + i) ^ ev
        gradient = grad_ref[pl.ds(i * rows, rows), :]
        change, prev_step, precond = terms(gradient, hist_ref, k)
        weighted = precond * change
        parts = (prev_step * change, prev_step * gradient, weighted * gradient, weighted * change)
        for n, part in enumerate(parts):
            total[n] = total[n] + jnp.sum(part.reshape(rows // 8, 8, LANES), axis=0)
    for n in range(4):
        out_ref[pl.ds(n, 1), :] = jnp.sum(total[n], axis=0, keepdims=True)
    out_ref[pl.ds(4, 4), :] = jnp.zeros((4, LANES), jnp.float32)


def direction_kernel(rows, evs, mine_ref, other_ref, hist_ref, *refs):
    sum_refs, (inv_ref, round_ref, grad_ref) = refs[:-3], refs[-3:]
    ev = lax.axis_index("ev")
    level = [ref[...] for ref in sum_refs]
    while len(level) > 1:
        level = [level[i] + level[i + 1] for i in range(0, len(level), 2)]
    sums = jnp.sum(level[0], axis=1, keepdims=True)
    curvature, slope, cross_term, self_term = (sums[n : n + 1] for n in range(4))
    alpha = slope / curvature
    beta = (cross_term - alpha * self_term) / curvature
    bend = alpha - beta
    half_rows = mine_ref.shape[0]
    for ref, part in ((mine_ref, ev & 1), (other_ref, 1 - (ev & 1))):
        grad_ref[pl.ds(pl.multiple_of(part * half_rows, 8), half_rows), :] = ref[...]
    for k in range(evs):
        at = pl.ds(pl.multiple_of((ev ^ k) * rows, ROW), rows)
        gradient = grad_ref[at, :]
        change, prev_step, precond = terms(gradient, hist_ref, k)
        scaled = precond * (gradient - alpha * change)
        direction = -(scaled + bend * prev_step)
        round_ref[at, :] = direction.astype(jnp.bfloat16)
        if k == 0:
            inv_ref[...] = direction


def unpack_kernel(comps, group, in_ref, out_ref, wide_ref):
    for s in range(group):
        wide_ref[pl.ds(s * PITCH, comps), :] = in_ref[pl.ds(s * comps, comps), :]
    for c in range(comps):
        out_ref[c, 0] = wide_ref[pl.ds(c, group, stride=PITCH), :]


def in_smem():
    return pl.BlockSpec(memory_space=pltpu.SMEM)


def in_vmem():
    return pl.BlockSpec(memory_space=pltpu.VMEM)


def in_hbm():
    return pl.BlockSpec(memory_space=pltpu.HBM)


def limit(mib):
    return pltpu.CompilerParams(vmem_limit_bytes=mib << 20)


def f32(*shape):
    return jax.ShapeDtypeStruct(shape, jnp.float32)


def bf16(*shape):
    return jax.ShapeDtypeStruct(shape, jnp.bfloat16)


def body(
    kernels, tile_owner, tile_source, tile_target, tile_seed, tile_count, prev_gradient,
    prev_step, precond,
):
    events, comps, eblocks, nodes = kernels.shape
    parts = lax.axis_size("mesh")
    evs = lax.axis_size("ev")
    group = precond.shape[2]
    subs = group * evs
    blocks = parts * subs
    half = parts // 2
    rows = comps * group
    part_rows = comps * subs
    tiles = tile_source.shape[1]
    dims = dict(field=kernels.shape, half=half, subs=subs, blocks=blocks, tiles=tiles)

    def swap(x, axis, k):
        size = parts if axis == "mesh" else evs
        return lax.ppermute(x, axis, [(i, i ^ k) for i in range(size)])

    owners = jnp.transpose(tile_owner, (0, 2, 1))
    counts = jnp.transpose(tile_count)
    table = bf16(SHAPES * nodes, nodes)
    code_rows = (CODES * events * tiles // LANES, LANES)
    codes_shape = jax.ShapeDtypeStruct(code_rows, jnp.int32)

    packed = pl.pallas_call(
        functools.partial(pack_kernel, comps, group),
        out_shape=f32(3, rows, nodes),
        in_specs=[in_vmem()] * 3,
        out_specs=in_vmem(),
        scratch_shapes=[pltpu.VMEM((group * PITCH, nodes), jnp.float32)],
        compiler_params=limit(2),
        name="pack",
    )(prev_gradient, prev_step, precond)
    hist = packed[None]
    for bit in range(evs.bit_length() - 1):
        hist = jnp.concatenate([hist, swap(hist, "ev", 1 << bit)], axis=0)

    tab = pl.pallas_call(
        functools.partial(table_kernel, nodes),
        out_shape=table,
        out_specs=in_vmem(),
        compiler_params=limit(1),
        cost_estimate=pl.CostEstimate(flops=1 << 28, bytes_accessed=4 << 20, transcendentals=0),
        name="table",
    )()
    sums, codes = pl.pallas_call(
        functools.partial(forward_kernel, dims),
        out_shape=[f32(blocks * comps + ROW, nodes), codes_shape],
        in_specs=[in_smem()] + [in_vmem()] * 6,
        out_specs=[in_vmem()] * 2,
        scratch_shapes=[
            pltpu.VMEM((events * eblocks * PITCH + ROW, nodes), jnp.float32),
            pltpu.SMEM(code_rows, jnp.int32),
            pltpu.SemaphoreType.DMA((1,)),
        ],
        compiler_params=limit(20),
        cost_estimate=pl.CostEstimate(
            flops=2 * events * tiles * ROW * nodes * nodes * 64,
            bytes_accessed=16 << 20,
            transcendentals=0,
        ),
        name="forward",
    )(counts, owners, tile_target, tile_source, tile_seed, kernels, tab)

    keep = sums[: half * part_rows].reshape(half, part_rows, nodes)
    send = sums[half * part_rows : 2 * half * part_rows].reshape(half, part_rows, nodes)
    got = swap(send, "mesh", 1)
    held = [None] + [keep[j] + got[j] for j in range(1, half)]
    arrived = []
    for j in range(1, half):
        arrived.append(swap(held[j], "mesh", 2 * j))
    total = pl.pallas_call(
        fold_kernel,
        out_shape=f32(part_rows, nodes),
        in_specs=[in_vmem()] * 2,
        out_specs=in_vmem(),
        compiler_params=limit(2),
        name="fold",
    )(keep[0], got[0])
    half_rows = part_rows // 2
    stay, go = pl.pallas_call(
        merge_kernel,
        out_shape=[f32(half_rows, nodes)] * 2,
        in_specs=[in_vmem()] * half,
        out_specs=[in_vmem()] * 2,
        compiler_params=limit(4),
        name="merge",
    )(total, *arrived)
    total, across = stay, swap(go, "ev", 1)
    for bit in range(1, evs.bit_length() - 1):
        total = total + across
        across = swap(total, "ev", 1 << bit)

    gradient, local = pl.pallas_call(
        functools.partial(sums_kernel, rows, evs),
        out_shape=[f32(half_rows, nodes), f32(8, nodes)],
        in_specs=[in_vmem()] * 3,
        out_specs=[in_vmem()] * 2,
        compiler_params=limit(4),
        name="sums",
    )(total, across, hist)
    local = local + swap(local, "ev", 1)
    gradient_other = swap(gradient, "ev", 1)
    local = local + swap(local, "mesh", 1)
    spread = [local] + [swap(local, "mesh", 2 * j) for j in range(1, half)]
    inverse, rounded = pl.pallas_call(
        functools.partial(direction_kernel, rows, evs),
        out_shape=[f32(rows, nodes), bf16(part_rows, nodes)],
        in_specs=[in_vmem()] * (3 + half),
        out_specs=[in_vmem()] * 2,
        scratch_shapes=[pltpu.VMEM((part_rows, nodes), jnp.float32)],
        compiler_params=limit(4),
        name="direction",
    )(gradient, gradient_other, hist, *spread)
    inversion_direction = pl.pallas_call(
        functools.partial(unpack_kernel, comps, group),
        out_shape=f32(*precond.shape),
        in_specs=[in_vmem()],
        out_specs=in_vmem(),
        scratch_shapes=[pltpu.VMEM((group * PITCH, nodes), jnp.float32)],
        compiler_params=limit(2),
        name="unpack",
    )(inverse)

    mine = [rounded]
    for j in range(1, half):
        mine.append(swap(rounded, "mesh", 2 * j))
    other = swap(jnp.stack(mine), "mesh", 1)

    event_direction = pl.pallas_call(
        functools.partial(backward_kernel, dims),
        out_shape=f32(*kernels.shape),
        in_specs=[in_smem()] + [in_vmem()] * (half + 3),
        out_specs=in_hbm(),
        scratch_shapes=[
            pltpu.VMEM((blocks * comps + ROW, nodes), jnp.float32),
            pltpu.VMEM((events * eblocks * PITCH + ROW, nodes), jnp.float32),
            pltpu.VMEM(kernels.shape, jnp.float32),
            pltpu.SMEM(code_rows, jnp.int32),
            pltpu.SemaphoreType.DMA((1 + events,)),
        ],
        compiler_params=limit(24),
        name="backward",
    )(counts, codes, tab, *mine, other)
    return inversion_direction, event_direction


def solution(mesh):
    in_specs = (
        P("ev", None, "mesh", None),
        P("ev", "mesh", None),
        P("ev", "mesh"),
        P("ev", "mesh"),
        P("ev", "mesh"),
        P("ev", "mesh"),
        P(None, "mesh", "ev", None),
        P(None, "mesh", "ev", None),
        P(None, "mesh", "ev", None),
    )
    out_specs = (P(None, "mesh", "ev", None), P("ev", None, "mesh", None))

    return jax.shard_map(body, mesh=mesh, in_specs=in_specs, out_specs=out_specs, check_vma=False)
```

```python
import functools
import math

import jax
import jax.numpy as jnp
import numpy as np
from jax import lax
from jax.experimental import pallas as pl
from jax.experimental.pallas import tpu as pltpu
from jax.sharding import PartitionSpec as P


OFFSETS = 7
SPREADS = 3
WEIGHTS = 4
SHAPES = OFFSETS * SPREADS * WEIGHTS
ROW = 16
PITCH = 13
LANES = 128
BAND = 16
CODES = 4
BODY = 2


def table_kernel(nodes, tab_ref):
    row = lax.broadcasted_iota(jnp.int32, (8, nodes), 0)
    lane = lax.broadcasted_iota(jnp.int32, (8, nodes), 1)
    signed = jnp.where(lane < nodes // 2, lane, lane - nodes)

    def one(k, carry):
        spread = 0.55 + 0.1 * k.astype(jnp.float32)
        for o in range(OFFSETS):
            distance = (row - signed - (o - OFFSETS // 2)).astype(jnp.float32)
            base = jnp.exp(-distance * distance / (2.0 * spread * spread))
            bells = []
            for i in range(0, nodes, 8):
                bell = base if i == 0 else pltpu.roll(base, i, 1)
                if i < 2 * BAND or i >= nodes - 2 * BAND:
                    near = jnp.abs(row + i - lane) < nodes // 2
                    bell = jnp.where(near, bell, 0.0)
                bells.append(bell)
            for w in range(WEIGHTS):
                weight = np.float32(0.1) + np.float32(0.1) * np.float32(w)
                first = (k + w * SPREADS) * (OFFSETS * nodes) + o * nodes
                for i in range(0, len(bells), 2):
                    pair = jnp.concatenate([weight * bells[i], weight * bells[i + 1]], axis=0)
                    at = pl.ds(pl.multiple_of(first + i * 8, ROW), ROW)
                    tab_ref[at, :] = pair.astype(jnp.bfloat16)
        return carry

    lax.fori_loop(0, SPREADS, one, 0)


def fill_codes(dims, counts, owner_ref, target_ref, source_ref, seed_ref, codes_ref):
    events, comps, eblocks, nodes = dims["field"]
    half, subs, blocks = dims["half"], dims["subs"], dims["blocks"]
    groups = dims["tiles"] // LANES
    lists = events * groups
    me = lax.axis_index("mesh")
    lane = lax.broadcasted_iota(jnp.int32, (1, LANES), 1)
    for v in range(events):
        for g in range(groups):
            at = pl.ds(g * LANES, LANES)
            live = lane + g * LANES < counts[v]
            r = owner_ref[v, :, at] ^ me
            slot = ((r & 1) * half + (r >> 1)) * subs + target_ref[pl.ds(v, 1), at]
            source = source_ref[pl.ds(v, 1), at] + v * eblocks
            seed = seed_ref[pl.ds(v, 1), at]
            turned = 2 * OFFSETS * ((seed * 9363) >> 16) - seed + (OFFSETS - 1)
            codes = (
                jnp.where(live, source, events * eblocks) * PITCH,
                jnp.where(live, slot, blocks) * comps,
                seed * nodes,
                turned * nodes,
            )
            for n, code in enumerate(codes):
                codes_ref[pl.ds(n * lists + v * groups + g, 1), :] = code


def tile_loop(v, count, groups, load, add):
    body = math.gcd(BODY, groups)

    def group(i, carry):
        first = v * groups + i * body
        places = [(first + p, u) for p in range(body) for u in range(LANES)]
        results = []
        for n in range(0, len(places), 2):
            x0, g0 = load(*places[n])
            x1, g1 = load(*places[n + 1])
            y = jnp.dot(
                jnp.concatenate([x0, x1], axis=0),
                jnp.concatenate([g0, g1], axis=1),
                preferred_element_type=jnp.float32,
            )
            results += [y[:ROW, :LANES], y[ROW:, LANES:]]
        for place, y in zip(places, results):
            add(*place, y)
        return carry

    size = body * LANES
    lax.fori_loop(0, (count + size - 1) // size, group, 0)


def forward_kernel(
    dims, count_ref, owner_ref, target_ref, source_ref, seed_ref, field_ref, tab_ref,
    sum_ref, codes_ref, rows_ref, code_ref, sems,
):
    events, comps, eblocks, nodes = dims["field"]
    groups = dims["tiles"] // LANES
    lists = events * groups
    counts = [count_ref[0, v] for v in range(events)]
    fill_codes(dims, counts, owner_ref, target_ref, source_ref, seed_ref, codes_ref)
    sum_ref[...] = jnp.zeros_like(sum_ref)
    to_smem = pltpu.make_async_copy(codes_ref, code_ref, sems.at[0])
    to_smem.start()
    for v in range(events):
        for c in range(comps):
            rows_ref[pl.ds(v * eblocks * PITCH + c, eblocks, stride=PITCH), :] = field_ref[
                v, c
            ].astype(jnp.float32)
    to_smem.wait()

    def load(i, u):
        shape = pl.multiple_of(code_ref[2 * lists + i, u], nodes)
        x = rows_ref[pl.ds(code_ref[i, u], ROW), :]
        return x.astype(jnp.bfloat16), tab_ref[pl.ds(shape, nodes), :]

    def add(i, u, y):
        at = pl.ds(pl.multiple_of(code_ref[lists + i, u], 4), comps)
        y = y.astype(jnp.bfloat16).astype(jnp.float32)
        sum_ref[at, :] = sum_ref[at, :] + y[:comps]

    for v in range(events):
        tile_loop(v, counts[v], groups, load, add)


def backward_kernel(dims, count_ref, codes_in, tab_ref, *refs):
    events, comps, eblocks, nodes = dims["field"]
    half, subs = dims["half"], dims["subs"]
    groups = dims["tiles"] // LANES
    lists = events * groups
    mine_refs, (other_ref, out_ref, rows_ref, sum_ref, tile_ref, code_ref, sems) = (
        refs[:half], refs[half:],
    )
    to_smem = pltpu.make_async_copy(codes_in, code_ref, sems.at[0])
    to_smem.start()
    sum_ref[...] = jnp.zeros_like(sum_ref)
    part = subs * comps
    for j in range(half):
        rows_ref[pl.ds(j * part, part), :] = mine_refs[j][...].astype(jnp.float32)
        rows_ref[pl.ds((half + j) * part, part), :] = other_ref[j].astype(jnp.float32)
    to_smem.wait()

    def load(i, u):
        shape = pl.multiple_of(code_ref[3 * lists + i, u], nodes)
        x = rows_ref[pl.ds(pl.multiple_of(code_ref[lists + i, u], 4), ROW), :]
        return x.astype(jnp.bfloat16), tab_ref[pl.ds(shape, nodes), :]

    def add(i, u, y):
        at = pl.ds(code_ref[i, u], comps)
        sum_ref[at, :] = sum_ref[at, :] + y[:comps]

    sends = []
    for v in range(events):
        tile_loop(v, count_ref[0, v], groups, load, add)
        for c in range(comps):
            tile_ref[v, c] = sum_ref[pl.ds(v * eblocks * PITCH + c, eblocks, stride=PITCH), :]
            sem = sems.at[1 + v * comps + c]
            send = pltpu.make_async_copy(tile_ref.at[v, c], out_ref.at[v, c], sem)
            send.start()
            sends.append(send)
    for send in sends:
        send.wait()


def pack_kernel(comps, group, *refs):
    ins, (out_ref, wide_ref) = refs[:-2], refs[-2:]
    for n, ref in enumerate(ins):
        for c in range(comps):
            wide_ref[pl.ds(c, group, stride=PITCH), :] = ref[c, 0]
        for s in range(group):
            out_ref[n, pl.ds(s * comps, comps), :] = wide_ref[pl.ds(s * PITCH, comps), :]


def fold_kernel(a_ref, b_ref, out_ref):
    out_ref[...] = a_ref[...] + b_ref[...]


def merge_kernel(*refs):
    ins, (stay_ref, go_ref) = refs[:-2], refs[-2:]
    rows = stay_ref.shape[0]
    odd = lax.axis_index("ev") & 1
    for out_ref, part in ((stay_ref, odd), (go_ref, 1 - odd)):
        at = pl.ds(pl.multiple_of(part * rows, 8), rows)
        total = ins[0][at, :]
        for ref in ins[1:]:
            total = total + ref[at, :]
        out_ref[...] = total


def terms(gradient, hist_ref, k):
    prev_gradient, prev_step, precond = hist_ref[k, 0], hist_ref[k, 1], hist_ref[k, 2]
    return gradient - prev_gradient, prev_step, precond


def sums_kernel(rows, evs, a_ref, b_ref, hist_ref, grad_ref, out_ref):
    ev = lax.axis_index("ev")
    grad_ref[...] = a_ref[...] + b_ref[...]
    total = [jnp.zeros((8, LANES), jnp.float32) for _ in range(4)]
    for i in range(evs // 2):
        k = ((ev & 1) * (evs // 2) + i) ^ ev
        gradient = grad_ref[pl.ds(i * rows, rows), :]
        change, prev_step, precond = terms(gradient, hist_ref, k)
        weighted = precond * change
        parts = (prev_step * change, prev_step * gradient, weighted * gradient, weighted * change)
        for n, part in enumerate(parts):
            total[n] = total[n] + jnp.sum(part.reshape(rows // 8, 8, LANES), axis=0)
    for n in range(4):
        out_ref[pl.ds(n, 1), :] = jnp.sum(total[n], axis=0, keepdims=True)
    out_ref[pl.ds(4, 4), :] = jnp.zeros((4, LANES), jnp.float32)


def direction_kernel(rows, evs, mine_ref, other_ref, hist_ref, *refs):
    sum_refs, (inv_ref, round_ref, grad_ref) = refs[:-3], refs[-3:]
    ev = lax.axis_index("ev")
    level = [ref[...] for ref in sum_refs]
    while len(level) > 1:
        level = [level[i] + level[i + 1] for i in range(0, len(level), 2)]
    sums = jnp.sum(level[0], axis=1, keepdims=True)
    curvature, slope, cross_term, self_term = (sums[n : n + 1] for n in range(4))
    alpha = slope / curvature
    beta = (cross_term - alpha * self_term) / curvature
    bend = alpha - beta
    half_rows = mine_ref.shape[0]
    for ref, part in ((mine_ref, ev & 1), (other_ref, 1 - (ev & 1))):
        grad_ref[pl.ds(pl.multiple_of(part * half_rows, 8), half_rows), :] = ref[...]
    for k in range(evs):
        at = pl.ds(pl.multiple_of((ev ^ k) * rows, ROW), rows)
        gradient = grad_ref[at, :]
        change, prev_step, precond = terms(gradient, hist_ref, k)
        scaled = precond * (gradient - alpha * change)
        direction = -(scaled + bend * prev_step)
        round_ref[at, :] = direction.astype(jnp.bfloat16)
        if k == 0:
            inv_ref[...] = direction


def unpack_kernel(comps, group, in_ref, out_ref, wide_ref):
    for s in range(group):
        wide_ref[pl.ds(s * PITCH, comps), :] = in_ref[pl.ds(s * comps, comps), :]
    for c in range(comps):
        out_ref[c, 0] = wide_ref[pl.ds(c, group, stride=PITCH), :]


def in_smem():
    return pl.BlockSpec(memory_space=pltpu.SMEM)


def in_vmem():
    return pl.BlockSpec(memory_space=pltpu.VMEM)


def in_hbm():
    return pl.BlockSpec(memory_space=pltpu.HBM)


def limit(mib):
    return pltpu.CompilerParams(vmem_limit_bytes=mib << 20)


def f32(*shape):
    return jax.ShapeDtypeStruct(shape, jnp.float32)


def bf16(*shape):
    return jax.ShapeDtypeStruct(shape, jnp.bfloat16)


def body(
    kernels, tile_owner, tile_source, tile_target, tile_seed, tile_count, prev_gradient,
    prev_step, precond,
):
    events, comps, eblocks, nodes = kernels.shape
    parts = lax.axis_size("mesh")
    evs = lax.axis_size("ev")
    group = precond.shape[2]
    subs = group * evs
    blocks = parts * subs
    half = parts // 2
    rows = comps * group
    part_rows = comps * subs
    tiles = tile_source.shape[1]
    dims = dict(field=kernels.shape, half=half, subs=subs, blocks=blocks, tiles=tiles)

    def swap(x, axis, k):
        size = parts if axis == "mesh" else evs
        return lax.ppermute(x, axis, [(i, i ^ k) for i in range(size)])

    owners = jnp.transpose(tile_owner, (0, 2, 1))
    counts = jnp.transpose(tile_count)
    table = bf16(SHAPES * nodes, nodes)
    code_rows = (CODES * events * tiles // LANES, LANES)
    codes_shape = jax.ShapeDtypeStruct(code_rows, jnp.int32)

    packed = pl.pallas_call(
        functools.partial(pack_kernel, comps, group),
        out_shape=f32(3, rows, nodes),
        in_specs=[in_vmem()] * 3,
        out_specs=in_vmem(),
        scratch_shapes=[pltpu.VMEM((group * PITCH, nodes), jnp.float32)],
        compiler_params=limit(2),
        name="pack",
    )(prev_gradient, prev_step, precond)
    hist = packed[None]
    for bit in range(evs.bit_length() - 1):
        hist = jnp.concatenate([hist, swap(hist, "ev", 1 << bit)], axis=0)

    tab = pl.pallas_call(
        functools.partial(table_kernel, nodes),
        out_shape=table,
        out_specs=in_vmem(),
        compiler_params=limit(1),
        cost_estimate=pl.CostEstimate(flops=1 << 28, bytes_accessed=4 << 20, transcendentals=0),
        name="table",
    )()
    sums, codes = pl.pallas_call(
        functools.partial(forward_kernel, dims),
        out_shape=[f32(blocks * comps + ROW, nodes), codes_shape],
        in_specs=[in_smem()] + [in_vmem()] * 6,
        out_specs=[in_vmem()] * 2,
        scratch_shapes=[
            pltpu.VMEM((events * eblocks * PITCH + ROW, nodes), jnp.float32),
            pltpu.SMEM(code_rows, jnp.int32),
            pltpu.SemaphoreType.DMA((1,)),
        ],
        compiler_params=limit(20),
        cost_estimate=pl.CostEstimate(
            flops=2 * events * tiles * ROW * nodes * nodes * 64,
            bytes_accessed=16 << 20,
            transcendentals=0,
        ),
        name="forward",
    )(counts, owners, tile_target, tile_source, tile_seed, kernels, tab)

    keep = sums[: half * part_rows].reshape(half, part_rows, nodes)
    send = sums[half * part_rows : 2 * half * part_rows].reshape(half, part_rows, nodes)
    got = swap(send, "mesh", 1)
    held = [None] + [keep[j] + got[j] for j in range(1, half)]
    arrived = []
    for j in range(1, half):
        arrived.append(swap(held[j], "mesh", 2 * j))
    total = pl.pallas_call(
        fold_kernel,
        out_shape=f32(part_rows, nodes),
        in_specs=[in_vmem()] * 2,
        out_specs=in_vmem(),
        compiler_params=limit(2),
        name="fold",
    )(keep[0], got[0])
    half_rows = part_rows // 2
    stay, go = pl.pallas_call(
        merge_kernel,
        out_shape=[f32(half_rows, nodes)] * 2,
        in_specs=[in_vmem()] * half,
        out_specs=[in_vmem()] * 2,
        compiler_params=limit(4),
        name="merge",
    )(total, *arrived)
    total, across = stay, swap(go, "ev", 1)
    for bit in range(1, evs.bit_length() - 1):
        total = total + across
        across = swap(total, "ev", 1 << bit)

    gradient, local = pl.pallas_call(
        functools.partial(sums_kernel, rows, evs),
        out_shape=[f32(half_rows, nodes), f32(8, nodes)],
        in_specs=[in_vmem()] * 3,
        out_specs=[in_vmem()] * 2,
        compiler_params=limit(4),
        name="sums",
    )(total, across, hist)
    across_both = [(i, i ^ (parts + 1)) for i in range(evs * parts)]
    by_ev = swap(local, "ev", 1)
    by_both = lax.ppermute(local, ("ev", "mesh"), across_both)
    by_core = swap(local, "mesh", 1)
    gradient_other = swap(gradient, "ev", 1)
    local = (local + by_core) + (by_ev + by_both)
    spread = [local] + [swap(local, "mesh", 2 * j) for j in range(1, half)]
    inverse, rounded = pl.pallas_call(
        functools.partial(direction_kernel, rows, evs),
        out_shape=[f32(rows, nodes), bf16(part_rows, nodes)],
        in_specs=[in_vmem()] * (3 + half),
        out_specs=[in_vmem()] * 2,
        scratch_shapes=[pltpu.VMEM((part_rows, nodes), jnp.float32)],
        compiler_params=limit(4),
        name="direction",
    )(gradient, gradient_other, hist, *spread)
    inversion_direction = pl.pallas_call(
        functools.partial(unpack_kernel, comps, group),
        out_shape=f32(*precond.shape),
        in_specs=[in_vmem()],
        out_specs=in_vmem(),
        scratch_shapes=[pltpu.VMEM((group * PITCH, nodes), jnp.float32)],
        compiler_params=limit(2),
        name="unpack",
    )(inverse)

    mine = [rounded]
    for j in range(1, half):
        mine.append(swap(rounded, "mesh", 2 * j))
    other = swap(jnp.stack(mine), "mesh", 1)

    event_direction = pl.pallas_call(
        functools.partial(backward_kernel, dims),
        out_shape=f32(*kernels.shape),
        in_specs=[in_smem()] + [in_vmem()] * (half + 3),
        out_specs=in_hbm(),
        scratch_shapes=[
            pltpu.VMEM((blocks * comps + ROW, nodes), jnp.float32),
            pltpu.VMEM((events * eblocks * PITCH + ROW, nodes), jnp.float32),
            pltpu.VMEM(kernels.shape, jnp.float32),
            pltpu.SMEM(code_rows, jnp.int32),
            pltpu.SemaphoreType.DMA((1 + events * comps,)),
        ],
        compiler_params=limit(24),
        name="backward",
    )(counts, codes, tab, *mine, other)
    return inversion_direction, event_direction


def solution(mesh):
    in_specs = (
        P("ev", None, "mesh", None),
        P("ev", "mesh", None),
        P("ev", "mesh"),
        P("ev", "mesh"),
        P("ev", "mesh"),
        P("ev", "mesh"),
        P(None, "mesh", "ev", None),
        P(None, "mesh", "ev", None),
        P(None, "mesh", "ev", None),
    )
    out_specs = (P(None, "mesh", "ev", None), P("ev", None, "mesh", None))

    return jax.shard_map(body, mesh=mesh, in_specs=in_specs, out_specs=out_specs, check_vma=False)
```

```python
import functools
import math

import jax
import jax.numpy as jnp
import numpy as np
from jax import lax
from jax.experimental import pallas as pl
from jax.experimental.pallas import tpu as pltpu
from jax.sharding import PartitionSpec as P


OFFSETS = 7
SPREADS = 3
WEIGHTS = 4
SHAPES = OFFSETS * SPREADS * WEIGHTS
ROW = 16
PITCH = 13
LANES = 128
BAND = 16
CODES = 4
BODY = 2


def table_kernel(nodes, tab_ref):
    row = lax.broadcasted_iota(jnp.int32, (8, nodes), 0)
    lane = lax.broadcasted_iota(jnp.int32, (8, nodes), 1)
    signed = jnp.where(lane < nodes // 2, lane, lane - nodes)

    def one(k, carry):
        spread = 0.55 + 0.1 * k.astype(jnp.float32)
        for o in range(OFFSETS):
            distance = (row - signed - (o - OFFSETS // 2)).astype(jnp.float32)
            base = jnp.exp(-distance * distance / (2.0 * spread * spread))
            bells = []
            for i in range(0, nodes, 8):
                bell = base if i == 0 else pltpu.roll(base, i, 1)
                if i < 2 * BAND or i >= nodes - 2 * BAND:
                    near = jnp.abs(row + i - lane) < nodes // 2
                    bell = jnp.where(near, bell, 0.0)
                bells.append(bell)
            for w in range(WEIGHTS):
                weight = np.float32(0.1) + np.float32(0.1) * np.float32(w)
                first = (k + w * SPREADS) * (OFFSETS * nodes) + o * nodes
                for i in range(0, len(bells), 2):
                    pair = jnp.concatenate([weight * bells[i], weight * bells[i + 1]], axis=0)
                    at = pl.ds(pl.multiple_of(first + i * 8, ROW), ROW)
                    tab_ref[at, :] = pair.astype(jnp.bfloat16)
        return carry

    lax.fori_loop(0, SPREADS, one, 0)


def turn(j, half):
    return (j & ~3) | ((j & 1) << 1) | ((j >> 1) & 1) if half > 2 else j


def fill_codes(dims, counts, owner_ref, target_ref, source_ref, seed_ref, codes_ref):
    events, comps, eblocks, nodes = dims["field"]
    half, subs, blocks = dims["half"], dims["subs"], dims["blocks"]
    groups = dims["tiles"] // LANES
    lists = events * groups
    me = lax.axis_index("mesh")
    lane = lax.broadcasted_iota(jnp.int32, (1, LANES), 1)
    for v in range(events):
        for g in range(groups):
            at = pl.ds(g * LANES, LANES)
            live = lane + g * LANES < counts[v]
            r = owner_ref[v, :, at] ^ me
            place = jnp.where(((r ^ me) & 1) == 1, turn(r >> 1, half), r >> 1)
            slot = ((r & 1) * half + place) * subs + target_ref[pl.ds(v, 1), at]
            source = source_ref[pl.ds(v, 1), at] + v * eblocks
            seed = seed_ref[pl.ds(v, 1), at]
            turned = 2 * OFFSETS * ((seed * 9363) >> 16) - seed + (OFFSETS - 1)
            codes = (
                jnp.where(live, source, events * eblocks) * PITCH,
                jnp.where(live, slot, blocks) * comps,
                seed * nodes,
                turned * nodes,
            )
            for n, code in enumerate(codes):
                codes_ref[pl.ds(n * lists + v * groups + g, 1), :] = code


def tile_loop(v, count, groups, load, add):
    body = math.gcd(BODY, groups)

    def group(i, carry):
        first = v * groups + i * body
        places = [(first + p, u) for p in range(body) for u in range(LANES)]
        results = []
        for n in range(0, len(places), 2):
            x0, g0 = load(*places[n])
            x1, g1 = load(*places[n + 1])
            y = jnp.dot(
                jnp.concatenate([x0, x1], axis=0),
                jnp.concatenate([g0, g1], axis=1),
                preferred_element_type=jnp.float32,
            )
            results += [y[:ROW, :LANES], y[ROW:, LANES:]]
        for place, y in zip(places, results):
            add(*place, y)
        return carry

    size = body * LANES
    lax.fori_loop(0, (count + size - 1) // size, group, 0)


def forward_kernel(
    dims, count_ref, owner_ref, target_ref, source_ref, seed_ref, field_ref, tab_ref,
    sum_ref, codes_ref, rows_ref, code_ref, sems,
):
    events, comps, eblocks, nodes = dims["field"]
    groups = dims["tiles"] // LANES
    lists = events * groups
    counts = [count_ref[0, v] for v in range(events)]
    fill_codes(dims, counts, owner_ref, target_ref, source_ref, seed_ref, codes_ref)
    sum_ref[...] = jnp.zeros_like(sum_ref)
    to_smem = pltpu.make_async_copy(codes_ref, code_ref, sems.at[0])
    to_smem.start()
    for v in range(events):
        for c in range(comps):
            rows_ref[pl.ds(v * eblocks * PITCH + c, eblocks, stride=PITCH), :] = field_ref[
                v, c
            ].astype(jnp.float32)
    to_smem.wait()

    def load(i, u):
        shape = pl.multiple_of(code_ref[2 * lists + i, u], nodes)
        x = rows_ref[pl.ds(code_ref[i, u], ROW), :]
        return x.astype(jnp.bfloat16), tab_ref[pl.ds(shape, nodes), :]

    def add(i, u, y):
        at = pl.ds(pl.multiple_of(code_ref[lists + i, u], 4), comps)
        y = y.astype(jnp.bfloat16).astype(jnp.float32)
        sum_ref[at, :] = sum_ref[at, :] + y[:comps]

    for v in range(events):
        tile_loop(v, counts[v], groups, load, add)


def backward_kernel(dims, count_ref, codes_in, tab_ref, *refs):
    events, comps, eblocks, nodes = dims["field"]
    half, subs = dims["half"], dims["subs"]
    groups = dims["tiles"] // LANES
    lists = events * groups
    mine_refs, (other_ref, out_ref, rows_ref, sum_ref, tile_ref, code_ref, sems) = (
        refs[:half], refs[half:],
    )
    to_smem = pltpu.make_async_copy(codes_in, code_ref, sems.at[0])
    to_smem.start()
    sum_ref[...] = jnp.zeros_like(sum_ref)
    part = subs * comps
    for j in range(half):
        rows_ref[pl.ds(j * part, part), :] = mine_refs[j][...].astype(jnp.float32)
        rows_ref[pl.ds((half + j) * part, part), :] = other_ref[j].astype(jnp.float32)
    to_smem.wait()

    def load(i, u):
        shape = pl.multiple_of(code_ref[3 * lists + i, u], nodes)
        x = rows_ref[pl.ds(pl.multiple_of(code_ref[lists + i, u], 4), ROW), :]
        return x.astype(jnp.bfloat16), tab_ref[pl.ds(shape, nodes), :]

    def add(i, u, y):
        at = pl.ds(code_ref[i, u], comps)
        sum_ref[at, :] = sum_ref[at, :] + y[:comps]

    sends = []
    for v in range(events):
        tile_loop(v, count_ref[0, v], groups, load, add)
        for c in range(comps):
            tile_ref[v, c] = sum_ref[pl.ds(v * eblocks * PITCH + c, eblocks, stride=PITCH), :]
            sem = sems.at[1 + v * comps + c]
            send = pltpu.make_async_copy(tile_ref.at[v, c], out_ref.at[v, c], sem)
            send.start()
            sends.append(send)
    for send in sends:
        send.wait()


def pack_kernel(comps, group, *refs):
    ins, (out_ref, wide_ref) = refs[:-2], refs[-2:]
    for n, ref in enumerate(ins):
        for c in range(comps):
            wide_ref[pl.ds(c, group, stride=PITCH), :] = ref[c, 0]
        for s in range(group):
            out_ref[n, pl.ds(s * comps, comps), :] = wide_ref[pl.ds(s * PITCH, comps), :]


def fold_kernel(a_ref, b_ref, out_ref):
    out_ref[...] = a_ref[...] + b_ref[...]


def add_kernel_call(a, b):
    return pl.pallas_call(
        fold_kernel,
        out_shape=f32(*a.shape),
        in_specs=[in_vmem()] * 2,
        out_specs=in_vmem(),
        compiler_params=limit(2),
    )(a, b)


def merge_kernel(*refs):
    ins, (stay_ref, go_ref) = refs[:-2], refs[-2:]
    rows = stay_ref.shape[0]
    odd = lax.axis_index("ev") & 1
    for out_ref, part in ((stay_ref, odd), (go_ref, 1 - odd)):
        at = pl.ds(pl.multiple_of(part * rows, 8), rows)
        total = ins[0][at, :]
        for ref in ins[1:]:
            total = total + ref[at, :]
        out_ref[...] = total


def terms(gradient, hist_ref, k):
    prev_gradient, prev_step, precond = hist_ref[k, 0], hist_ref[k, 1], hist_ref[k, 2]
    return gradient - prev_gradient, prev_step, precond


def sums_kernel(rows, evs, a_ref, b_ref, hist_ref, grad_ref, out_ref):
    ev = lax.axis_index("ev")
    grad_ref[...] = a_ref[...] + b_ref[...]
    total = [jnp.zeros((8, LANES), jnp.float32) for _ in range(4)]
    for i in range(evs // 2):
        k = ((ev & 1) * (evs // 2) + i) ^ ev
        gradient = grad_ref[pl.ds(i * rows, rows), :]
        change, prev_step, precond = terms(gradient, hist_ref, k)
        weighted = precond * change
        parts = (prev_step * change, prev_step * gradient, weighted * gradient, weighted * change)
        for n, part in enumerate(parts):
            total[n] = total[n] + jnp.sum(part.reshape(rows // 8, 8, LANES), axis=0)
    for n in range(4):
        out_ref[pl.ds(n, 1), :] = jnp.sum(total[n], axis=0, keepdims=True)
    out_ref[pl.ds(4, 4), :] = jnp.zeros((4, LANES), jnp.float32)


def direction_kernel(rows, evs, mine_ref, other_ref, hist_ref, *refs):
    sum_refs, (inv_ref, round_ref, grad_ref) = refs[:-3], refs[-3:]
    ev = lax.axis_index("ev")
    level = [ref[...] for ref in sum_refs]
    while len(level) > 1:
        level = [level[i] + level[i + 1] for i in range(0, len(level), 2)]
    sums = jnp.sum(level[0], axis=1, keepdims=True)
    curvature, slope, cross_term, self_term = (sums[n : n + 1] for n in range(4))
    alpha = slope / curvature
    beta = (cross_term - alpha * self_term) / curvature
    bend = alpha - beta
    half_rows = mine_ref.shape[0]
    for ref, part in ((mine_ref, ev & 1), (other_ref, 1 - (ev & 1))):
        grad_ref[pl.ds(pl.multiple_of(part * half_rows, 8), half_rows), :] = ref[...]
    for k in range(evs):
        at = pl.ds(pl.multiple_of((ev ^ k) * rows, ROW), rows)
        gradient = grad_ref[at, :]
        change, prev_step, precond = terms(gradient, hist_ref, k)
        scaled = precond * (gradient - alpha * change)
        direction = -(scaled + bend * prev_step)
        round_ref[at, :] = direction.astype(jnp.bfloat16)
        if k == 0:
            inv_ref[...] = direction


def unpack_kernel(comps, group, in_ref, out_ref, wide_ref):
    for s in range(group):
        wide_ref[pl.ds(s * PITCH, comps), :] = in_ref[pl.ds(s * comps, comps), :]
    for c in range(comps):
        out_ref[c, 0] = wide_ref[pl.ds(c, group, stride=PITCH), :]


def in_smem():
    return pl.BlockSpec(memory_space=pltpu.SMEM)


def in_vmem():
    return pl.BlockSpec(memory_space=pltpu.VMEM)


def in_hbm():
    return pl.BlockSpec(memory_space=pltpu.HBM)


def limit(mib):
    return pltpu.CompilerParams(vmem_limit_bytes=mib << 20)


def f32(*shape):
    return jax.ShapeDtypeStruct(shape, jnp.float32)


def bf16(*shape):
    return jax.ShapeDtypeStruct(shape, jnp.bfloat16)


def body(
    kernels, tile_owner, tile_source, tile_target, tile_seed, tile_count, prev_gradient,
    prev_step, precond,
):
    events, comps, eblocks, nodes = kernels.shape
    parts = lax.axis_size("mesh")
    evs = lax.axis_size("ev")
    group = precond.shape[2]
    subs = group * evs
    blocks = parts * subs
    half = parts // 2
    rows = comps * group
    part_rows = comps * subs
    tiles = tile_source.shape[1]
    dims = dict(field=kernels.shape, half=half, subs=subs, blocks=blocks, tiles=tiles)

    def swap(x, axis, k):
        size = parts if axis == "mesh" else evs
        return lax.ppermute(x, axis, [(i, i ^ k) for i in range(size)])

    owners = jnp.transpose(tile_owner, (0, 2, 1))
    counts = jnp.transpose(tile_count)
    table = bf16(SHAPES * nodes, nodes)
    code_rows = (CODES * events * tiles // LANES, LANES)
    codes_shape = jax.ShapeDtypeStruct(code_rows, jnp.int32)

    packed = pl.pallas_call(
        functools.partial(pack_kernel, comps, group),
        out_shape=f32(3, rows, nodes),
        in_specs=[in_vmem()] * 3,
        out_specs=in_vmem(),
        scratch_shapes=[pltpu.VMEM((group * PITCH, nodes), jnp.float32)],
        compiler_params=limit(2),
        name="pack",
    )(prev_gradient, prev_step, precond)
    hist = packed[None]
    for bit in range(evs.bit_length() - 1):
        hist = jnp.concatenate([hist, swap(hist, "ev", 1 << bit)], axis=0)

    def along(x, j):
        pairs = [(i, i ^ 2 * (turn(j, half) if i & 1 else j)) for i in range(parts)]
        return lax.ppermute(x, "mesh", pairs)

    tab = pl.pallas_call(
        functools.partial(table_kernel, nodes),
        out_shape=table,
        out_specs=in_vmem(),
        compiler_params=limit(1),
        cost_estimate=pl.CostEstimate(flops=1 << 28, bytes_accessed=4 << 20, transcendentals=0),
        name="table",
    )()
    sums, codes = pl.pallas_call(
        functools.partial(forward_kernel, dims),
        out_shape=[f32(blocks * comps + ROW, nodes), codes_shape],
        in_specs=[in_smem()] + [in_vmem()] * 6,
        out_specs=[in_vmem()] * 2,
        scratch_shapes=[
            pltpu.VMEM((events * eblocks * PITCH + ROW, nodes), jnp.float32),
            pltpu.SMEM(code_rows, jnp.int32),
            pltpu.SemaphoreType.DMA((1,)),
        ],
        compiler_params=limit(20),
        cost_estimate=pl.CostEstimate(
            flops=2 * events * tiles * ROW * nodes * nodes * 64,
            bytes_accessed=16 << 20,
            transcendentals=0,
        ),
        name="forward",
    )(counts, owners, tile_target, tile_source, tile_seed, kernels, tab)

    keep = sums[: half * part_rows].reshape(half, part_rows, nodes)
    send = sums[half * part_rows : 2 * half * part_rows].reshape(half, part_rows, nodes)
    got = swap(send, "mesh", 1)
    held = [None] + [keep[j] + got[j] for j in range(1, half)]
    for h in range(4, half, 4):
        far = swap(jnp.stack(held[h : h + 4]), "mesh", 2 * h)
        held[1:4] = [held[j] + far[j] for j in range(1, 4)]
        keep = keep.at[0].add(far[0])
    arrived = []
    if half > 2:
        corner = along(held[3], 1)
        arrived.append(along(held[1], 1))
        relay = add_kernel_call(held[2], corner)
        arrived.append(along(relay, 2))
    else:
        arrived += [along(held[j], j) for j in range(1, half)]
    total = add_kernel_call(keep[0], got[0])
    half_rows = part_rows // 2
    stay, go = pl.pallas_call(
        merge_kernel,
        out_shape=[f32(half_rows, nodes)] * 2,
        in_specs=[in_vmem()] * (1 + len(arrived)),
        out_specs=[in_vmem()] * 2,
        compiler_params=limit(4),
        name="merge",
    )(total, *arrived)
    total, across = stay, swap(go, "ev", 1)
    for bit in range(1, evs.bit_length() - 1):
        total = total + across
        across = swap(total, "ev", 1 << bit)

    gradient, local = pl.pallas_call(
        functools.partial(sums_kernel, rows, evs),
        out_shape=[f32(half_rows, nodes), f32(8, nodes)],
        in_specs=[in_vmem()] * 3,
        out_specs=[in_vmem()] * 2,
        compiler_params=limit(4),
        name="sums",
    )(total, across, hist)
    across_both = [(i, i ^ (parts + 1)) for i in range(evs * parts)]
    by_ev = swap(local, "ev", 1)
    by_both = lax.ppermute(local, ("ev", "mesh"), across_both)
    by_core = swap(local, "mesh", 1)
    gradient_other = swap(gradient, "ev", 1)
    local = (local + by_core) + (by_ev + by_both)
    spread = [local] + [swap(local, "mesh", 2 * j) for j in range(1, half)]
    inverse, rounded = pl.pallas_call(
        functools.partial(direction_kernel, rows, evs),
        out_shape=[f32(rows, nodes), bf16(part_rows, nodes)],
        in_specs=[in_vmem()] * (3 + half),
        out_specs=[in_vmem()] * 2,
        scratch_shapes=[pltpu.VMEM((part_rows, nodes), jnp.float32)],
        compiler_params=limit(4),
        name="direction",
    )(gradient, gradient_other, hist, *spread)
    inversion_direction = pl.pallas_call(
        functools.partial(unpack_kernel, comps, group),
        out_shape=f32(*precond.shape),
        in_specs=[in_vmem()],
        out_specs=in_vmem(),
        scratch_shapes=[pltpu.VMEM((group * PITCH, nodes), jnp.float32)],
        compiler_params=limit(2),
        name="unpack",
    )(inverse)

    mine = [rounded]
    for j in range(1, half):
        mine.append(along(rounded, j))
    other = swap(jnp.stack(mine), "mesh", 1)

    event_direction = pl.pallas_call(
        functools.partial(backward_kernel, dims),
        out_shape=f32(*kernels.shape),
        in_specs=[in_smem()] + [in_vmem()] * (half + 3),
        out_specs=in_hbm(),
        scratch_shapes=[
            pltpu.VMEM((blocks * comps + ROW, nodes), jnp.float32),
            pltpu.VMEM((events * eblocks * PITCH + ROW, nodes), jnp.float32),
            pltpu.VMEM(kernels.shape, jnp.float32),
            pltpu.SMEM(code_rows, jnp.int32),
            pltpu.SemaphoreType.DMA((1 + events * comps,)),
        ],
        compiler_params=limit(24),
        name="backward",
    )(counts, codes, tab, *mine, other)
    return inversion_direction, event_direction


def solution(mesh):
    in_specs = (
        P("ev", None, "mesh", None),
        P("ev", "mesh", None),
        P("ev", "mesh"),
        P("ev", "mesh"),
        P("ev", "mesh"),
        P("ev", "mesh"),
        P(None, "mesh", "ev", None),
        P(None, "mesh", "ev", None),
        P(None, "mesh", "ev", None),
    )
    out_specs = (P(None, "mesh", "ev", None), P("ev", None, "mesh", None))

    return jax.shard_map(body, mesh=mesh, in_specs=in_specs, out_specs=out_specs, check_vma=False)
```

```python
import functools
import math

import jax
import jax.numpy as jnp
import numpy as np
from jax import lax
from jax.experimental import pallas as pl
from jax.experimental.pallas import tpu as pltpu
from jax.sharding import PartitionSpec as P


OFFSETS = 7
SPREADS = 3
WEIGHTS = 4
SHAPES = OFFSETS * SPREADS * WEIGHTS
ROW = 16
PITCH = 13
LANES = 128
BAND = 16
CODES = 4
BODY = 2


def table_kernel(nodes, tab_ref):
    row = lax.broadcasted_iota(jnp.int32, (8, nodes), 0)
    lane = lax.broadcasted_iota(jnp.int32, (8, nodes), 1)
    signed = jnp.where(lane < nodes // 2, lane, lane - nodes)

    def one(k, carry):
        spread = 0.55 + 0.1 * k.astype(jnp.float32)
        for o in range(OFFSETS):
            distance = (row - signed - (o - OFFSETS // 2)).astype(jnp.float32)
            base = jnp.exp(-distance * distance / (2.0 * spread * spread))
            bells = []
            for i in range(0, nodes, 8):
                bell = base if i == 0 else pltpu.roll(base, i, 1)
                if i < 2 * BAND or i >= nodes - 2 * BAND:
                    near = jnp.abs(row + i - lane) < nodes // 2
                    bell = jnp.where(near, bell, 0.0)
                bells.append(bell)
            for w in range(WEIGHTS):
                weight = np.float32(0.1) + np.float32(0.1) * np.float32(w)
                first = (k + w * SPREADS) * (OFFSETS * nodes) + o * nodes
                for i in range(0, len(bells), 2):
                    pair = jnp.concatenate([weight * bells[i], weight * bells[i + 1]], axis=0)
                    at = pl.ds(pl.multiple_of(first + i * 8, ROW), ROW)
                    tab_ref[at, :] = pair.astype(jnp.bfloat16)
        return carry

    lax.fori_loop(0, SPREADS, one, 0)


def turn(j, half):
    return (j & ~3) | ((j & 1) << 1) | ((j >> 1) & 1) if half > 2 else j


def fill_codes(dims, counts, owner_ref, target_ref, source_ref, seed_ref, codes_ref):
    events, comps, eblocks, nodes = dims["field"]
    half, subs, blocks = dims["half"], dims["subs"], dims["blocks"]
    groups = dims["tiles"] // LANES
    lists = events * groups
    me = lax.axis_index("mesh")
    lane = lax.broadcasted_iota(jnp.int32, (1, LANES), 1)
    for v in range(events):
        for g in range(groups):
            at = pl.ds(g * LANES, LANES)
            live = lane + g * LANES < counts[v]
            r = owner_ref[v, :, at] ^ me
            place = jnp.where(((r ^ me) & 1) == 1, turn(r >> 1, half), r >> 1)
            slot = ((r & 1) * half + place) * subs + target_ref[pl.ds(v, 1), at]
            source = source_ref[pl.ds(v, 1), at] + v * eblocks
            seed = seed_ref[pl.ds(v, 1), at]
            turned = 2 * OFFSETS * ((seed * 9363) >> 16) - seed + (OFFSETS - 1)
            codes = (
                jnp.where(live, source, events * eblocks) * PITCH,
                jnp.where(live, slot, blocks) * comps,
                seed * nodes,
                turned * nodes,
            )
            for n, code in enumerate(codes):
                codes_ref[pl.ds(n * lists + v * groups + g, 1), :] = code


def tile_loop(v, count, groups, load, add):
    body = math.gcd(BODY, groups)

    def group(i, carry):
        first = v * groups + i * body
        places = [(first + p, u) for p in range(body) for u in range(LANES)]
        results = []
        for n in range(0, len(places), 2):
            x0, g0 = load(*places[n])
            x1, g1 = load(*places[n + 1])
            y = jnp.dot(
                jnp.concatenate([x0, x1], axis=0),
                jnp.concatenate([g0, g1], axis=1),
                preferred_element_type=jnp.float32,
            )
            results += [y[:ROW, :LANES], y[ROW:, LANES:]]
        for place, y in zip(places, results):
            add(*place, y)
        return carry

    size = body * LANES
    lax.fori_loop(0, (count + size - 1) // size, group, 0)


def forward_kernel(
    dims, count_ref, owner_ref, target_ref, source_ref, seed_ref, field_ref, tab_ref,
    sum_ref, codes_ref, rows_ref, code_ref, sems,
):
    events, comps, eblocks, nodes = dims["field"]
    groups = dims["tiles"] // LANES
    lists = events * groups
    counts = [count_ref[0, v] for v in range(events)]
    fill_codes(dims, counts, owner_ref, target_ref, source_ref, seed_ref, codes_ref)
    sum_ref[...] = jnp.zeros_like(sum_ref)
    to_smem = pltpu.make_async_copy(codes_ref, code_ref, sems.at[0])
    to_smem.start()
    for v in range(events):
        for c in range(comps):
            rows_ref[pl.ds(v * eblocks * PITCH + c, eblocks, stride=PITCH), :] = field_ref[
                v, c
            ].astype(jnp.float32)
    to_smem.wait()

    def load(i, u):
        shape = pl.multiple_of(code_ref[2 * lists + i, u], nodes)
        x = rows_ref[pl.ds(code_ref[i, u], ROW), :]
        return x.astype(jnp.bfloat16), tab_ref[pl.ds(shape, nodes), :]

    def add(i, u, y):
        at = pl.ds(pl.multiple_of(code_ref[lists + i, u], 4), comps)
        y = y.astype(jnp.bfloat16).astype(jnp.float32)
        sum_ref[at, :] = sum_ref[at, :] + y[:comps]

    for v in range(events):
        tile_loop(v, counts[v], groups, load, add)


def backward_kernel(dims, count_ref, codes_in, tab_ref, *refs):
    events, comps, eblocks, nodes = dims["field"]
    half, subs = dims["half"], dims["subs"]
    groups = dims["tiles"] // LANES
    lists = events * groups
    mine_refs, (other_ref, out_ref, rows_ref, sum_ref, tile_ref, code_ref, sems) = (
        refs[:half], refs[half:],
    )
    to_smem = pltpu.make_async_copy(codes_in, code_ref, sems.at[0])
    to_smem.start()
    sum_ref[...] = jnp.zeros_like(sum_ref)
    part = subs * comps
    for j in range(half):
        rows_ref[pl.ds(j * part, part), :] = mine_refs[j][...].astype(jnp.float32)
        rows_ref[pl.ds((half + j) * part, part), :] = other_ref[j].astype(jnp.float32)
    to_smem.wait()

    def load(i, u):
        shape = pl.multiple_of(code_ref[3 * lists + i, u], nodes)
        x = rows_ref[pl.ds(pl.multiple_of(code_ref[lists + i, u], 4), ROW), :]
        return x.astype(jnp.bfloat16), tab_ref[pl.ds(shape, nodes), :]

    def add(i, u, y):
        at = pl.ds(code_ref[i, u], comps)
        sum_ref[at, :] = sum_ref[at, :] + y[:comps]

    sends = []
    for v in range(events):
        tile_loop(v, count_ref[0, v], groups, load, add)
        for c in range(comps):
            tile_ref[v, c] = sum_ref[pl.ds(v * eblocks * PITCH + c, eblocks, stride=PITCH), :]
            sem = sems.at[1 + v * comps + c]
            send = pltpu.make_async_copy(tile_ref.at[v, c], out_ref.at[v, c], sem)
            send.start()
            sends.append(send)
    for send in sends:
        send.wait()


def pack_kernel(comps, group, *refs):
    ins, (out_ref, wide_ref) = refs[:-2], refs[-2:]
    for n, ref in enumerate(ins):
        for c in range(comps):
            wide_ref[pl.ds(c, group, stride=PITCH), :] = ref[c, 0]
        for s in range(group):
            out_ref[n, pl.ds(s * comps, comps), :] = wide_ref[pl.ds(s * PITCH, comps), :]


def fold_kernel(a_ref, b_ref, out_ref):
    out_ref[...] = a_ref[...] + b_ref[...]


def slots_kernel(first, sum_ref, got_ref, *out_refs):
    for n, out_ref in enumerate(out_refs):
        rows = out_ref.shape[0]
        out_ref[...] = sum_ref[pl.ds((first + n) * rows, rows), :] + got_ref[n]


def add_kernel_call(a, b):
    return pl.pallas_call(
        fold_kernel,
        out_shape=f32(*a.shape),
        in_specs=[in_vmem()] * 2,
        out_specs=in_vmem(),
        compiler_params=limit(2),
    )(a, b)


def merge_kernel(*refs):
    ins, (stay_ref, go_ref) = refs[:-2], refs[-2:]
    rows = stay_ref.shape[0]
    odd = lax.axis_index("ev") & 1
    for out_ref, part in ((stay_ref, odd), (go_ref, 1 - odd)):
        at = pl.ds(pl.multiple_of(part * rows, 8), rows)
        total = ins[0][at, :]
        for ref in ins[1:]:
            total = total + ref[at, :]
        out_ref[...] = total


def terms(gradient, hist_ref, k):
    prev_gradient, prev_step, precond = hist_ref[k, 0], hist_ref[k, 1], hist_ref[k, 2]
    return gradient - prev_gradient, prev_step, precond


def sums_kernel(rows, evs, a_ref, b_ref, hist_ref, grad_ref, out_ref):
    ev = lax.axis_index("ev")
    grad_ref[...] = a_ref[...] + b_ref[...]
    total = [jnp.zeros((8, LANES), jnp.float32) for _ in range(4)]
    for i in range(evs // 2):
        k = ((ev & 1) * (evs // 2) + i) ^ ev
        gradient = grad_ref[pl.ds(i * rows, rows), :]
        change, prev_step, precond = terms(gradient, hist_ref, k)
        weighted = precond * change
        parts = (prev_step * change, prev_step * gradient, weighted * gradient, weighted * change)
        for n, part in enumerate(parts):
            total[n] = total[n] + jnp.sum(part.reshape(rows // 8, 8, LANES), axis=0)
    for n in range(4):
        out_ref[pl.ds(n, 1), :] = jnp.sum(total[n], axis=0, keepdims=True)
    out_ref[pl.ds(4, 4), :] = jnp.zeros((4, LANES), jnp.float32)


def direction_kernel(rows, evs, mine_ref, other_ref, hist_ref, *refs):
    sum_refs, (inv_ref, round_ref, grad_ref) = refs[:-3], refs[-3:]
    ev = lax.axis_index("ev")
    level = [ref[...] for ref in sum_refs]
    while len(level) > 1:
        level = [level[i] + level[i + 1] for i in range(0, len(level), 2)]
    sums = jnp.sum(level[0], axis=1, keepdims=True)
    curvature, slope, cross_term, self_term = (sums[n : n + 1] for n in range(4))
    alpha = slope / curvature
    beta = (cross_term - alpha * self_term) / curvature
    bend = alpha - beta
    half_rows = mine_ref.shape[0]
    for ref, part in ((mine_ref, ev & 1), (other_ref, 1 - (ev & 1))):
        grad_ref[pl.ds(pl.multiple_of(part * half_rows, 8), half_rows), :] = ref[...]
    for k in range(evs):
        at = pl.ds(pl.multiple_of((ev ^ k) * rows, ROW), rows)
        gradient = grad_ref[at, :]
        change, prev_step, precond = terms(gradient, hist_ref, k)
        scaled = precond * (gradient - alpha * change)
        direction = -(scaled + bend * prev_step)
        round_ref[at, :] = direction.astype(jnp.bfloat16)
        if k == 0:
            inv_ref[...] = direction


def unpack_kernel(comps, group, in_ref, out_ref, wide_ref):
    for s in range(group):
        wide_ref[pl.ds(s * PITCH, comps), :] = in_ref[pl.ds(s * comps, comps), :]
    for c in range(comps):
        out_ref[c, 0] = wide_ref[pl.ds(c, group, stride=PITCH), :]


def in_smem():
    return pl.BlockSpec(memory_space=pltpu.SMEM)


def in_vmem():
    return pl.BlockSpec(memory_space=pltpu.VMEM)


def in_hbm():
    return pl.BlockSpec(memory_space=pltpu.HBM)


def limit(mib):
    return pltpu.CompilerParams(vmem_limit_bytes=mib << 20)


def f32(*shape):
    return jax.ShapeDtypeStruct(shape, jnp.float32)


def bf16(*shape):
    return jax.ShapeDtypeStruct(shape, jnp.bfloat16)


def body(
    kernels, tile_owner, tile_source, tile_target, tile_seed, tile_count, prev_gradient,
    prev_step, precond,
):
    events, comps, eblocks, nodes = kernels.shape
    parts = lax.axis_size("mesh")
    evs = lax.axis_size("ev")
    group = precond.shape[2]
    subs = group * evs
    blocks = parts * subs
    half = parts // 2
    rows = comps * group
    part_rows = comps * subs
    tiles = tile_source.shape[1]
    dims = dict(field=kernels.shape, half=half, subs=subs, blocks=blocks, tiles=tiles)

    def swap(x, axis, k):
        size = parts if axis == "mesh" else evs
        return lax.ppermute(x, axis, [(i, i ^ k) for i in range(size)])

    owners = jnp.transpose(tile_owner, (0, 2, 1))
    counts = jnp.transpose(tile_count)
    table = bf16(SHAPES * nodes, nodes)
    code_rows = (CODES * events * tiles // LANES, LANES)
    codes_shape = jax.ShapeDtypeStruct(code_rows, jnp.int32)

    packed = pl.pallas_call(
        functools.partial(pack_kernel, comps, group),
        out_shape=f32(3, rows, nodes),
        in_specs=[in_vmem()] * 3,
        out_specs=in_vmem(),
        scratch_shapes=[pltpu.VMEM((group * PITCH, nodes), jnp.float32)],
        compiler_params=limit(2),
        name="pack",
    )(prev_gradient, prev_step, precond)
    hist = packed[None]
    for bit in range(evs.bit_length() - 1):
        hist = jnp.concatenate([hist, swap(hist, "ev", 1 << bit)], axis=0)

    def along(x, j):
        pairs = [(i, i ^ 2 * (turn(j, half) if i & 1 else j)) for i in range(parts)]
        return lax.ppermute(x, "mesh", pairs)

    tab = pl.pallas_call(
        functools.partial(table_kernel, nodes),
        out_shape=table,
        out_specs=in_vmem(),
        compiler_params=limit(1),
        cost_estimate=pl.CostEstimate(flops=1 << 28, bytes_accessed=4 << 20, transcendentals=0),
        name="table",
    )()
    sums, codes = pl.pallas_call(
        functools.partial(forward_kernel, dims),
        out_shape=[f32(blocks * comps + ROW, nodes), codes_shape],
        in_specs=[in_smem()] + [in_vmem()] * 6,
        out_specs=[in_vmem()] * 2,
        scratch_shapes=[
            pltpu.VMEM((events * eblocks * PITCH + ROW, nodes), jnp.float32),
            pltpu.SMEM(code_rows, jnp.int32),
            pltpu.SemaphoreType.DMA((1,)),
        ],
        compiler_params=limit(20),
        cost_estimate=pl.CostEstimate(
            flops=2 * events * tiles * ROW * nodes * nodes * 64,
            bytes_accessed=16 << 20,
            transcendentals=0,
        ),
        name="forward",
    )(counts, owners, tile_target, tile_source, tile_seed, kernels, tab)

    keep = sums[: half * part_rows].reshape(half, part_rows, nodes)
    send = sums[half * part_rows : 2 * half * part_rows].reshape(half, part_rows, nodes)

    def slots_plus(got, first):
        count = got.shape[0]
        return pl.pallas_call(
            functools.partial(slots_kernel, first),
            out_shape=[f32(part_rows, nodes)] * count,
            in_specs=[in_vmem()] * 2,
            out_specs=[in_vmem()] * count,
            compiler_params=limit(4),
        )(sums, got)

    if half == 4:
        first = swap(send[3:], "mesh", 1)
        got = swap(send[:3], "mesh", 1)
        held = slots_plus(got, 0) + slots_plus(first, 3)
        base = held[0]
    else:
        got = swap(send, "mesh", 1)
        held = [None] + [keep[j] + got[j] for j in range(1, half)]
        for h in range(4, half, 4):
            far = swap(jnp.stack(held[h : h + 4]), "mesh", 2 * h)
            held[1:4] = [held[j] + far[j] for j in range(1, 4)]
            keep = keep.at[0].add(far[0])
        base = add_kernel_call(keep[0], got[0])
    arrived = []
    if half > 2:
        corner = along(held[3], 1)
        arrived.append(along(held[1], 1))
        relay = add_kernel_call(held[2], corner)
        arrived.append(along(relay, 2))
    else:
        arrived += [along(held[j], j) for j in range(1, half)]
    total = base
    half_rows = part_rows // 2
    stay, go = pl.pallas_call(
        merge_kernel,
        out_shape=[f32(half_rows, nodes)] * 2,
        in_specs=[in_vmem()] * (1 + len(arrived)),
        out_specs=[in_vmem()] * 2,
        compiler_params=limit(4),
        name="merge",
    )(total, *arrived)
    total, across = stay, swap(go, "ev", 1)
    for bit in range(1, evs.bit_length() - 1):
        total = total + across
        across = swap(total, "ev", 1 << bit)

    gradient, local = pl.pallas_call(
        functools.partial(sums_kernel, rows, evs),
        out_shape=[f32(half_rows, nodes), f32(8, nodes)],
        in_specs=[in_vmem()] * 3,
        out_specs=[in_vmem()] * 2,
        compiler_params=limit(4),
        name="sums",
    )(total, across, hist)
    across_both = [(i, i ^ (parts + 1)) for i in range(evs * parts)]
    by_ev = swap(local, "ev", 1)
    by_both = lax.ppermute(local, ("ev", "mesh"), across_both)
    by_core = swap(local, "mesh", 1)
    gradient_other = swap(gradient, "ev", 1)
    local = (local + by_core) + (by_ev + by_both)
    spread = [local] + [swap(local, "mesh", 2 * j) for j in range(1, half)]
    inverse, rounded = pl.pallas_call(
        functools.partial(direction_kernel, rows, evs),
        out_shape=[f32(rows, nodes), bf16(part_rows, nodes)],
        in_specs=[in_vmem()] * (3 + half),
        out_specs=[in_vmem()] * 2,
        scratch_shapes=[pltpu.VMEM((part_rows, nodes), jnp.float32)],
        compiler_params=limit(4),
        name="direction",
    )(gradient, gradient_other, hist, *spread)
    inversion_direction = pl.pallas_call(
        functools.partial(unpack_kernel, comps, group),
        out_shape=f32(*precond.shape),
        in_specs=[in_vmem()],
        out_specs=in_vmem(),
        scratch_shapes=[pltpu.VMEM((group * PITCH, nodes), jnp.float32)],
        compiler_params=limit(2),
        name="unpack",
    )(inverse)

    mine = [rounded]
    for j in range(1, half):
        mine.append(along(rounded, j))
    other = swap(jnp.stack(mine), "mesh", 1)

    event_direction = pl.pallas_call(
        functools.partial(backward_kernel, dims),
        out_shape=f32(*kernels.shape),
        in_specs=[in_smem()] + [in_vmem()] * (half + 3),
        out_specs=in_hbm(),
        scratch_shapes=[
            pltpu.VMEM((blocks * comps + ROW, nodes), jnp.float32),
            pltpu.VMEM((events * eblocks * PITCH + ROW, nodes), jnp.float32),
            pltpu.VMEM(kernels.shape, jnp.float32),
            pltpu.SMEM(code_rows, jnp.int32),
            pltpu.SemaphoreType.DMA((1 + events * comps,)),
        ],
        compiler_params=limit(24),
        name="backward",
    )(counts, codes, tab, *mine, other)
    return inversion_direction, event_direction


def solution(mesh):
    in_specs = (
        P("ev", None, "mesh", None),
        P("ev", "mesh", None),
        P("ev", "mesh"),
        P("ev", "mesh"),
        P("ev", "mesh"),
        P("ev", "mesh"),
        P(None, "mesh", "ev", None),
        P(None, "mesh", "ev", None),
        P(None, "mesh", "ev", None),
    )
    out_specs = (P(None, "mesh", "ev", None), P("ev", None, "mesh", None))

    return jax.shard_map(
        body, mesh=mesh, in_specs=in_specs, out_specs=out_specs, check_vma=False
    )
```
